32 devices in a mesh: seq: 8 (over z, y), chan: 4 (over x, core).
Axes of the slice: x: 2, y: 2, z: 4, core: 2. Of those that a mesh axis runs over, the one named last changes fastest.
Arguments:
- features: bfloat16 [2048, 3, 8192], P(('seq', 'chan')), may hold values from -6 to 6
- cotangent: bfloat16 [2048, 8192], P('seq', 'chan'), may hold values from -6 to 6
- short_filter: float32 [3, 512, 7], P(None, 'chan'), may hold values from -2.5 to 2.5
- medium_filter: float32 [512, 128], P('chan'), may hold values from -0.5 to 0.5
- doc_start: int32 [8], replicated, may hold values from 0 to 255
Outputs:
- hyena_out: bfloat16 [2048, 8192], P('seq', 'chan')
- feature_grad: bfloat16 [2048, 3, 8192], P(('seq', 'chan'))
The draws below stay inside these ranges and needn't reach their ends.
Inputs may be any that keep to these rules, and one draw needn't show every extreme that they name: Each shard holds exactly one document start, at position doc_start[i] of its 256 positions.
All inputs are finite; a program needn't handle non-finite values.
Results may differ from the reference program's by a relative error of at most 0.006.
Values may be sent and summed in bfloat16 or wider, within the bound.
A program may use at most 128 MiB of HBM per device.

```python
import jax
import jax.numpy as jnp
from jax import lax

D = 8192
GROUPS = 512
SHORT = 7
MEDIUM = 128
TOK_DEV = 256
TOKENS = 2048
SHARDS = 8


def with_ends(array, key, smallest, largest):
    shape = array.shape
    index_at = [jax.random.randint(jax.random.fold_in(key, axis), (), 0, shape[axis]) for axis in range(len(shape))]
    array = array.at[tuple(index_at)].set(smallest)
    longest = shape.index(max(shape))
    index_at[longest] = (index_at[longest] + 1) % shape[longest]
    return array.at[tuple(index_at)].set(largest)


def shard_levels(own_key, shape, cuts, least, top_value):
    level, own = 1.0, jax.random.fold_in(own_key, 6)
    for position, shards_of in cuts:
        draws = jnp.exp(jax.random.uniform(jax.random.fold_in(own, position), (shards_of,), jnp.float32, least / len(cuts), top_value / len(cuts)))
        level = level * jnp.repeat(draws, shape[position] // shards_of).reshape([-1 if axis == position else 1 for axis in range(len(shape))])
    return level


def normal_values(own_key, extent, deviation, reach, shards=(), kind=jnp.bfloat16):
    level = shard_levels(own_key, extent, shards, -0.22, 0.18) if shards else 1.0
    drawn = jax.random.normal(own_key, extent, jnp.float32) * deviation * level
    return jnp.minimum(jnp.maximum(drawn, -reach), reach).astype(kind)


def setup_inputs(seed: int = 0) -> dict:
    key_list = jax.random.split(jax.random.key(seed), 6)
    return {
        "features": normal_values(key_list[0], (TOKENS, 3, D), 1.0, 6.0, ((0, 32),)),
        "cotangent": normal_values(key_list[1], (TOKENS, D), 1.0, 6.0, ((0, 8), (1, 4))),
        "short_filter": normal_values(key_list[2], (3, GROUPS, SHORT), 0.4, 2.5, ((1, 4),), jnp.float32),
        "medium_filter": normal_values(key_list[3], (GROUPS, MEDIUM), MEDIUM ** -0.5, 0.5, ((0, 4),), jnp.float32),
        "doc_start": with_ends(jax.random.randint(key_list[4], (SHARDS,), 0, TOK_DEV), jax.random.fold_in(key_list[4], 1), 0, TOK_DEV - 1).astype(jnp.int32),
    }


ref_block = 128
ref_groups = 32


def doc_ids(doc_start):
    shard_count = doc_start.shape[0]
    bounds = jnp.arange(shard_count, dtype=jnp.int32) * TOK_DEV + doc_start.astype(jnp.int32)
    marks = jnp.zeros((shard_count * TOK_DEV,), jnp.int32).at[bounds].add(1)
    return jnp.cumsum(marks).astype(jnp.int32)


def short_forward(source, chan_taps, doc_index):
    row_count = source.shape[0]
    running = jnp.zeros(source.shape, jnp.float32)
    for offset in range(SHORT):
        shifted = jnp.pad(source[:row_count - offset], ((offset, 0), (0, 0), (0, 0)))
        open_tap = jnp.concatenate([jnp.zeros((offset,), bool), doc_index[:row_count - offset] == doc_index[offset:]])
        running = running + jnp.where(open_tap[:, None, None], chan_taps[None, :, :, offset] * shifted.astype(jnp.float32), 0.0)
    return running


def short_backward(grad_short, chan_taps, doc_index):
    row_count = grad_short.shape[0]
    running = jnp.zeros(grad_short.shape, jnp.float32)
    for offset in range(SHORT):
        shifted = jnp.pad(grad_short[offset:], ((0, offset), (0, 0), (0, 0)))
        open_tap = jnp.concatenate([doc_index[offset:] == doc_index[:row_count - offset], jnp.zeros((offset,), bool)])
        running = running + jnp.where(open_tap[:, None, None], chan_taps[None, :, :, offset] * shifted, 0.0)
    return running


def band_forward(gated, group_filter, doc_index):
    row_count, batch_width = gated.shape
    group_count = group_filter.shape[0]
    group_width = batch_width // group_count
    padded = jnp.concatenate([jnp.zeros((MEDIUM, batch_width), gated.dtype), gated], axis=0)
    padded_ids = jnp.concatenate([jnp.full((MEDIUM,), -1, jnp.int32), doc_index])
    lag_steps = jnp.arange(ref_block, dtype=jnp.int32)[:, None] + MEDIUM - jnp.arange(ref_block + MEDIUM, dtype=jnp.int32)[None, :]
    inside = (lag_steps >= 0) & (lag_steps < MEDIUM)
    lag_table = jnp.where(inside[None], jnp.take(group_filter, jnp.clip(lag_steps, 0, MEDIUM - 1), axis=1), jnp.zeros((), group_filter.dtype))

    def one_block(row_start):
        window = lax.dynamic_slice_in_dim(padded, row_start, ref_block + MEDIUM, 0)
        window_ids = lax.dynamic_slice_in_dim(padded_ids, row_start, ref_block + MEDIUM, 0)
        target_ids = lax.dynamic_slice_in_dim(padded_ids, row_start + MEDIUM, ref_block, 0)
        band_matrix = jnp.where((target_ids[:, None] == window_ids[None, :])[None], lag_table, jnp.zeros((), lag_table.dtype))
        window = window.reshape(ref_block + MEDIUM, group_count, group_width)
        result = jnp.einsum("gts,sgc->tgc", band_matrix.astype(jnp.float32), window.astype(jnp.float32))
        return result.reshape(ref_block, batch_width)

    block_starts = (jnp.arange(row_count // ref_block) * ref_block).astype(jnp.int32)
    return lax.map(one_block, block_starts).reshape(row_count, batch_width)


def band_backward(grad_long, group_filter, doc_index):
    row_count, batch_width = grad_long.shape
    group_count = group_filter.shape[0]
    group_width = batch_width // group_count
    padded = jnp.concatenate([grad_long, jnp.zeros((MEDIUM, batch_width), grad_long.dtype)], axis=0)
    padded_ids = jnp.concatenate([doc_index, jnp.full((MEDIUM,), -1, jnp.int32)])
    lag_steps = jnp.arange(ref_block + MEDIUM, dtype=jnp.int32)[None, :] - jnp.arange(ref_block, dtype=jnp.int32)[:, None]
    inside = (lag_steps >= 0) & (lag_steps < MEDIUM)
    lag_table = jnp.where(inside[None], jnp.take(group_filter, jnp.clip(lag_steps, 0, MEDIUM - 1), axis=1), jnp.zeros((), group_filter.dtype))

    def one_block(row_start):
        window = lax.dynamic_slice_in_dim(padded, row_start, ref_block + MEDIUM, 0)
        window_ids = lax.dynamic_slice_in_dim(padded_ids, row_start, ref_block + MEDIUM, 0)
        target_ids = lax.dynamic_slice_in_dim(padded_ids, row_start, ref_block, 0)
        band_matrix = jnp.where((target_ids[:, None] == window_ids[None, :])[None], lag_table, jnp.zeros((), lag_table.dtype))
        window = window.reshape(ref_block + MEDIUM, group_count, group_width)
        result = jnp.einsum("gts,sgc->tgc", band_matrix.astype(jnp.float32), window.astype(jnp.float32))
        return result.reshape(ref_block, batch_width)

    block_starts = (jnp.arange(row_count // ref_block) * ref_block).astype(jnp.int32)
    return lax.map(one_block, block_starts).reshape(row_count, batch_width)


def reference(features, cotangent, short_filter, medium_filter, doc_start):
    doc_index = doc_ids(doc_start)
    group_width = D // GROUPS
    batch_width = ref_groups * group_width
    row_count = features.shape[0]

    def group_work(batch_index):
        source = lax.dynamic_slice_in_dim(features, batch_index * batch_width, batch_width, 2)
        grad_out = lax.dynamic_slice_in_dim(cotangent, batch_index * batch_width, batch_width, 1)
        batch_taps = lax.dynamic_slice_in_dim(short_filter, batch_index * ref_groups, ref_groups, 1)
        chan_taps = jnp.repeat(batch_taps, group_width, axis=1)
        group_filter = lax.dynamic_slice_in_dim(medium_filter, batch_index * ref_groups, ref_groups, 0).astype(jnp.bfloat16)
        short_out = short_forward(source, chan_taps, doc_index)
        gated = (short_out[:, 1] * short_out[:, 2]).astype(jnp.bfloat16)
        long_conv = band_forward(gated, group_filter, doc_index)
        hyena_out = (short_out[:, 0] * long_conv).astype(jnp.bfloat16)
        grad_query = grad_out.astype(jnp.float32) * long_conv
        grad_long = (grad_out.astype(jnp.float32) * short_out[:, 0]).astype(jnp.bfloat16)
        grad_gated = band_backward(grad_long, group_filter, doc_index)
        grad_short = jnp.stack([grad_query, grad_gated * short_out[:, 2], grad_gated * short_out[:, 1]], axis=1)
        feature_grad = short_backward(grad_short, chan_taps, doc_index).astype(jnp.bfloat16)
        return hyena_out, feature_grad

    outs_all, grads_all = lax.map(group_work, jnp.arange(GROUPS // ref_groups, dtype=jnp.int32))
    hyena_out = jnp.transpose(outs_all, (1, 0, 2)).reshape(row_count, D)
    feature_grad = jnp.transpose(grads_all, (1, 2, 0, 3)).reshape(row_count, 3, D)
    return (hyena_out, feature_grad)
```

```python
import functools

import jax
import jax.numpy as jnp
from jax import lax
from jax.experimental import pallas as pl
from jax.experimental.pallas import tpu as pltpu
from jax.sharding import PartitionSpec as P

SHORT = 7
MEDIUM = 128
PAD = 144
TAIL = 16
LANES = 128
MESH = pl.DeviceIdType.MESH
ANY = pl.BlockSpec(memory_space=pl.ANY)


def greet(chans, seqs):
    c, s = lax.axis_index("chan"), lax.axis_index("seq")
    bar = pltpu.get_barrier_semaphore()
    for k in range(1, chans):
        pl.semaphore_signal(bar, inc=1, device_id={"chan": lax.rem(c + k, chans)}, device_id_type=MESH)
    count = chans - 1
    if seqs:
        for k in (1, seqs - 1):
            pl.semaphore_signal(bar, inc=1, device_id={"seq": lax.rem(s + k, seqs)}, device_id_type=MESH)
        count += 2
    pl.semaphore_wait(bar, count)


def gather_kernel(chans, seqs, x, cot, zero, ext, cext, ssem, rsem, lsem, hs, hr):
    c, s = lax.axis_index("chan"), lax.axis_index("seq")
    rows = x.shape[1]
    width = ext.shape[2]
    own = rows * chans
    greet(chans, seqs)

    def block(dst):
        return x.at[:, :, pl.ds(pl.multiple_of(dst * width, width), width)]

    def place(src):
        return ext.at[:, pl.ds(pl.multiple_of(PAD + src * rows, 16), rows), :]

    copies = []
    for k in range(1, chans):
        d = lax.rem(c + k, chans)
        cp = pltpu.make_async_remote_copy(
            block(d), place(c), ssem.at[k], rsem.at[k], device_id={"chan": d}, device_id_type=MESH)
        cp.start()
        copies.append(cp)
    local = [
        pltpu.make_async_copy(block(c), place(c), lsem.at[0]),
        pltpu.make_async_copy(cot, cext.at[pl.ds(0, own)], lsem.at[1]),
    ]
    for cp in local:
        cp.start()
    up, down = lax.rem(s + 1, seqs), lax.rem(s + seqs - 1, seqs)
    chead = pltpu.make_async_remote_copy(
        cot.at[pl.ds(0, PAD)], cext.at[pl.ds(own, PAD)], hs.at[0], hr.at[0],
        device_id={"seq": down}, device_id_type=MESH)
    tail = pltpu.make_async_remote_copy(
        ext.at[:, pl.ds(own, PAD)], ext.at[:, pl.ds(0, PAD)], hs.at[1], hr.at[1],
        device_id={"seq": up}, device_id_type=MESH)
    head = pltpu.make_async_remote_copy(
        ext.at[:, pl.ds(PAD, PAD)], ext.at[:, pl.ds(PAD + own, PAD)], hs.at[2], hr.at[2],
        device_id={"seq": down}, device_id_type=MESH)
    first, last = s == 0, s == seqs - 1
    zlo = pltpu.make_async_copy(zero, ext.at[:, pl.ds(0, PAD)], lsem.at[2])
    zhi = pltpu.make_async_copy(zero, ext.at[:, pl.ds(PAD + own, PAD)], lsem.at[3])
    zc = pltpu.make_async_copy(zero.at[0], cext.at[pl.ds(own, PAD)], lsem.at[4])

    @pl.when(jnp.logical_not(first))
    def _():
        chead.start()

    @pl.when(first)
    def _():
        zlo.start()

    @pl.when(last)
    def _():
        zhi.start()
        zc.start()

    for cp in copies:
        cp.wait_recv()
    local[0].wait()

    @pl.when(jnp.logical_not(last))
    def _():
        tail.start()

    @pl.when(jnp.logical_not(first))
    def _():
        head.start()

    @pl.when(jnp.logical_not(first))
    def _():
        chead.wait_send()
        head.wait_send()
        tail.wait_recv()

    @pl.when(jnp.logical_not(last))
    def _():
        tail.wait_send()
        chead.wait_recv()
        head.wait_recv()

    @pl.when(first)
    def _():
        zlo.wait()

    @pl.when(last)
    def _():
        zhi.wait()
        zc.wait()

    local[1].wait()
    for cp in copies:
        cp.wait_send()


def return_kernel(chans, x, out, ssem, rsem, lsem):
    c = lax.axis_index("chan")
    rows = out.shape[1]
    width = x.shape[2]
    greet(chans, 0)

    def block(dst):
        return x.at[:, pl.ds(pl.multiple_of(dst * rows, 16), rows), :]

    def place(src):
        return out.at[:, :, pl.ds(pl.multiple_of(src * width, width), width)]

    copies = []
    for k in range(1, chans):
        d = lax.rem(c + k, chans)
        cp = pltpu.make_async_remote_copy(
            block(d), place(c), ssem.at[k], rsem.at[k], device_id={"chan": d}, device_id_type=MESH)
        cp.start()
        copies.append(cp)
    local = pltpu.make_async_copy(block(c), place(c), lsem)
    local.start()
    local.wait()
    for cp in copies:
        cp.wait()


def mix_kernel(own, ext, cext, taps, filt, filt_rev, seg_col, seg_row, hy, fg,
               xs, fm, mf, mb, lf, lt, gat, gl, sh, gs):
    blocks = own // MEDIUM
    sizes = [MEDIUM] * blocks + [TAIL]
    grow = own + PAD

    @pl.when(pl.program_id(0) == 0)
    def _():
        for j in range(1, SHORT):
            n = fm.shape[1] - 8
            same = seg_col[pl.ds(8, n), :] == seg_col[pl.ds(8 - j, n), :]
            fm[j - 1, pl.ds(8, n), :] = jnp.where(same, 1.0, 0.0)
        for b, rows in enumerate(sizes):
            r = lax.broadcasted_iota(jnp.int32, (rows, 2 * MEDIUM), 0)
            k = lax.broadcasted_iota(jnp.int32, (rows, 2 * MEDIUM), 1)
            here = jnp.tile(seg_col[pl.ds(PAD + MEDIUM * b, rows), :], (1, 2))
            past = jnp.broadcast_to(seg_row[0:1, pl.ds(MEDIUM * b, 2 * MEDIUM)], (rows, 2 * MEDIUM))
            lag = r + MEDIUM - k
            ok = (lag >= 0) & (lag < MEDIUM) & (here == past)
            mf[b, pl.ds(0, rows), :] = jnp.where(ok, 1.0, 0.0).astype(jnp.bfloat16)
            ahead = jnp.broadcast_to(seg_row[0:1, pl.ds(MEDIUM * (b + 1), 2 * MEDIUM)], (rows, 2 * MEDIUM))
            lag = k - r
            ok = (lag >= 0) & (lag < MEDIUM) & (here == ahead)
            mb[b, pl.ds(0, rows), :] = jnp.where(ok, 1.0, 0.0).astype(jnp.bfloat16)
        gat[...] = jnp.zeros_like(gat)
        gl[...] = jnp.zeros_like(gl)

    xs[...] = ext[...].astype(jnp.float32)
    coef = [[taps[m, j : j + 1, :] for j in range(SHORT)] for m in range(3)]

    def short(m, start, rows):
        total = coef[m][0] * xs[m, pl.ds(start, rows), :]
        for j in range(1, SHORT):
            total = total + coef[m][j] * (
                fm[j - 1, pl.ds(start, rows), :] * xs[m, pl.ds(start - j, rows), :])
        return total

    step = 80
    for at in range(0, grow, step):
        q = short(0, PAD + at, step)
        if at < own + TAIL:
            n = min(step, own + TAIL - at)
            sh[0, pl.ds(at, n), :] = q[:n]
        gl[pl.ds(at, step), :] = (cext[pl.ds(at, step), :].astype(jnp.float32) * q).astype(jnp.bfloat16)
    for at in range(0, grow, step):
        k = short(1, PAD - MEDIUM + at, step)
        v = short(2, PAD - MEDIUM + at, step)
        gat[pl.ds(at, step), :] = (k * v).astype(jnp.bfloat16)
        lo = max(0, MEDIUM - at)
        if lo < step:
            sh[1, pl.ds(at + lo - MEDIUM, step - lo), :] = k[lo:]
            sh[2, pl.ds(at + lo - MEDIUM, step - lo), :] = v[lo:]

    lane_group = lax.broadcasted_iota(jnp.int32, (MEDIUM, LANES), 1) // (LANES // 8)

    def band(filters, masks):
        for g in range(8):
            row = jnp.broadcast_to(filters[g : g + 1, :], (MEDIUM, MEDIUM))
            circ = pltpu.roll(row, 0, 1, stride=1, stride_axis=0).astype(jnp.bfloat16)
            two = jnp.concatenate([circ, circ], axis=1)
            for b in range(blocks):
                lf[b, pl.ds(g * MEDIUM, MEDIUM), :] = two * masks[b]
            lt[pl.ds(g * TAIL, TAIL), :] = two[:TAIL] * masks[blocks, pl.ds(0, TAIL), :]

    def product(b, source):
        rhs = source[pl.ds(MEDIUM * b, 2 * MEDIUM), :]
        rows = sizes[b]
        lhs = lf[b] if b < blocks else lt[...]
        res = jnp.dot(lhs, rhs, preferred_element_type=jnp.float32)
        total = res[:rows]
        for g in range(1, 8):
            total = jnp.where(lane_group[:rows] == g, res[g * rows : (g + 1) * rows], total)
        return total

    band(filt_rev, mf)
    for b, rows in enumerate(sizes):
        long = product(b, gat)
        at = pl.ds(MEDIUM * b, rows)
        if b < blocks:
            hy[at, :] = (sh[0, at, :] * long).astype(jnp.bfloat16)
        gs[0, at, :] = cext[at, :].astype(jnp.float32) * long
    band(filt, mb)
    for b, rows in enumerate(sizes):
        back = product(b, gl)
        at = pl.ds(MEDIUM * b, rows)
        gs[1, at, :] = back * sh[2, at, :]
        gs[2, at, :] = back * sh[1, at, :]

    for m in range(3):
        for at in range(0, own, 64):
            total = coef[m][0] * gs[m, pl.ds(at, 64), :]
            for j in range(1, SHORT):
                total = total + coef[m][j] * (
                    fm[j - 1, pl.ds(PAD + at + j, 64), :] * gs[m, pl.ds(at + j, 64), :])
            fg[m, pl.ds(at, 64), :] = total.astype(jnp.bfloat16)


def solution(mesh):
    chans, seqs = mesh.shape["chan"], mesh.shape["seq"]

    def body(features, cotangent, short_filter, medium_filter, doc_start):
        own, width = cotangent.shape
        rows, _, full = features.shape
        groups = medium_filter.shape[0]
        grow = own + PAD
        total = own + 2 * PAD
        bf, f32 = jnp.bfloat16, jnp.float32
        x = jnp.transpose(features, (1, 0, 2))
        zero = jnp.zeros((3, PAD, width), bf)
        dma = pltpu.SemaphoreType.DMA
        ext, cext = pl.pallas_call(
            functools.partial(gather_kernel, chans, seqs),
            out_shape=(jax.ShapeDtypeStruct((3, total, width), bf), jax.ShapeDtypeStruct((grow, width), bf)),
            in_specs=[ANY] * 3,
            out_specs=(ANY, ANY),
            scratch_shapes=[dma((chans,)), dma((chans,)), dma((5,)), dma((3,)), dma((3,))],
            compiler_params=pltpu.CompilerParams(collective_id=0, has_side_effects=True),
            name="gather_parts",
        )(x, cotangent, zero)
        span = total + MEDIUM
        pos = lax.axis_index("seq") * own - PAD + jnp.arange(span, dtype=jnp.int32)
        bounds = jnp.arange(doc_start.shape[0], dtype=jnp.int32) * own + doc_start
        seg = jnp.sum((bounds[None, :] <= pos[:, None]).astype(jnp.int32), axis=1)
        seg_col = jnp.broadcast_to(seg[:total, None], (total, LANES))
        reach = own + 3 * MEDIUM
        seg_row = jnp.broadcast_to(seg[PAD - MEDIUM : PAD - MEDIUM + reach][None], (8, reach))
        taps = jnp.repeat(jnp.transpose(short_filter, (0, 2, 1)), width // groups, axis=2)
        taps = jnp.pad(taps, ((0, 0), (0, 1), (0, 0)))
        filt = medium_filter.astype(bf).astype(f32)
        filt_rev = jnp.roll(filt[:, ::-1], 1, axis=1)
        blocks = own // MEDIUM
        whole = lambda shape: pl.BlockSpec(shape, lambda i: (0,) * len(shape))
        hy, fg = pl.pallas_call(
            functools.partial(mix_kernel, own),
            grid=(width // LANES,),
            out_shape=(jax.ShapeDtypeStruct((own, width), bf), jax.ShapeDtypeStruct((3, own, width), bf)),
            in_specs=[
                pl.BlockSpec((3, total, LANES), lambda i: (0, 0, i)),
                pl.BlockSpec((grow, LANES), lambda i: (0, i)),
                pl.BlockSpec((3, 8, LANES), lambda i: (0, 0, i)),
                pl.BlockSpec((8, MEDIUM), lambda i: (i, 0)),
                pl.BlockSpec((8, MEDIUM), lambda i: (i, 0)),
                whole((total, LANES)),
                whole((8, reach)),
            ],
            out_specs=(
                pl.BlockSpec((own, LANES), lambda i: (0, i)),
                pl.BlockSpec((3, own, LANES), lambda i: (0, 0, i)),
            ),
            scratch_shapes=[
                pltpu.VMEM((3, total, LANES), f32),
                pltpu.VMEM((SHORT - 1, total, LANES), f32),
                pltpu.VMEM((blocks + 1, MEDIUM, 2 * MEDIUM), bf),
                pltpu.VMEM((blocks + 1, MEDIUM, 2 * MEDIUM), bf),
                pltpu.VMEM((blocks, 8 * MEDIUM, 2 * MEDIUM), bf),
                pltpu.VMEM((8 * TAIL, 2 * MEDIUM), bf),
                pltpu.VMEM((own + 2 * MEDIUM, LANES), bf),
                pltpu.VMEM((own + 2 * MEDIUM, LANES), bf),
                pltpu.VMEM((3, own + TAIL, LANES), f32),
                pltpu.VMEM((3, own + TAIL, LANES), f32),
            ],
            compiler_params=pltpu.CompilerParams(
                dimension_semantics=("arbitrary",), vmem_limit_bytes=40 << 20),
            name="mix_tile",
        )(ext, cext, taps, filt, filt_rev, seg_col, seg_row)
        back = pl.pallas_call(
            functools.partial(return_kernel, chans),
            out_shape=jax.ShapeDtypeStruct((3, rows, full), bf),
            in_specs=[ANY],
            out_specs=ANY,
            scratch_shapes=[dma((chans,)), dma((chans,)), dma],
            compiler_params=pltpu.CompilerParams(collective_id=1, has_side_effects=True),
            name="return_parts",
        )(fg)
        return hy, jnp.transpose(back, (1, 0, 2))

    in_specs = (
        P(("seq", "chan"), None, None),
        P("seq", "chan"),
        P(None, "chan", None),
        P("chan", None),
        P(),
    )
    out_specs = (P("seq", "chan"), P(("seq", "chan"), None, None))
    return jax.shard_map(body, mesh=mesh, in_specs=in_specs, out_specs=out_specs, check_vma=False)
```

```python
import functools

import jax
import jax.numpy as jnp
from jax import lax
from jax.experimental import pallas as pl
from jax.experimental.pallas import tpu as pltpu
from jax.sharding import PartitionSpec as P

SHORT = 7
MEDIUM = 128
EDGE = 8
TAIL = 16
GROW = MEDIUM + TAIL
LANES = 128
WIDE = 1024
FAR = 1 << 20
MESH = pl.DeviceIdType.MESH
ANY = pl.BlockSpec(memory_space=pl.ANY)


def spot():
    return lax.axis_index("chan"), lax.axis_index("seq")


def greet(chans, seqs, ring, line):
    c, s = spot()
    bar = pltpu.get_barrier_semaphore()
    for k in range(1, chans):
        pl.semaphore_signal(bar, inc=1, device_id={"chan": lax.rem(c + k, chans)}, device_id_type=MESH)
    count = chans - 1
    if ring:
        for k in (1, seqs - 1):
            pl.semaphore_signal(bar, inc=1, device_id={"seq": lax.rem(s + k, seqs)}, device_id_type=MESH)
        count += 2
    if line:
        for dev in line_ends(chans, seqs):
            pl.semaphore_signal(bar, inc=1, device_id=dev, device_id_type=MESH)
        count += 2
    pl.semaphore_wait(bar, count)


def line_ends(chans, seqs):
    c, s = spot()
    after = {"seq": lax.rem(s + (c + 1) // chans, seqs), "chan": lax.rem(c + 1, chans)}
    ahead = {"seq": lax.rem(s + seqs - 1 + (c + chans - 1) // chans, seqs), "chan": lax.rem(c + chans - 1, chans)}
    return after, ahead


def remote(src, dst, ssem, rsem, dev):
    return pltpu.make_async_remote_copy(src, dst, ssem, rsem, device_id=dev, device_id_type=MESH)


def first_kernel(chans, seqs, x, cot, ctaps, q, xprev, xnext, taps, cnext, ssem, rsem, tsem, usem, hs, hr, lsem):
    c, s = spot()
    rows = x.shape[1]
    width = q.shape[1]
    greet(chans, seqs, True, True)
    after, ahead = line_ends(chans, seqs)
    copies = [
        remote(x.at[pl.ds(1, 2), pl.ds(rows - EDGE, EDGE)], xprev, hs.at[0], hr.at[0], after),
        remote(x.at[pl.ds(1, 2), pl.ds(0, EDGE)], xnext, hs.at[1], hr.at[1], ahead),
        remote(cot.at[pl.ds(0, GROW)], cnext, hs.at[2], hr.at[2], {"seq": lax.rem(s + seqs - 1, seqs)}),
    ]
    for k in range(1, chans):
        d = lax.rem(c + k, chans)
        copies.append(remote(ctaps, taps.at[c], tsem.at[k], usem.at[k], {"chan": d}))
    place = q.at[pl.ds(pl.multiple_of(c * rows, 16), rows)]
    for k in range(1, chans):
        d = lax.rem(c + k, chans)
        part = x.at[0, :, pl.ds(pl.multiple_of(d * width, width), width)]
        copies.append(remote(part, place, ssem.at[k], rsem.at[k], {"chan": d}))
    mine = x.at[0, :, pl.ds(pl.multiple_of(c * width, width), width)]
    copies.append(pltpu.make_async_copy(mine, place, lsem.at[0]))
    copies.append(pltpu.make_async_copy(ctaps, taps.at[c], lsem.at[1]))
    for cp in copies:
        cp.start()
    for cp in copies:
        cp.wait()


def second_kernel(chans, seqs, q, gated, gown, gprev, gnext, qprev, qnext, ssem, rsem, hs, hr, lsem):
    c, s = spot()
    rows = gated.shape[0]
    own, width = q.shape
    greet(chans, seqs, True, False)
    up, down = {"seq": lax.rem(s + 1, seqs)}, {"seq": lax.rem(s + seqs - 1, seqs)}
    place = gown.at[pl.ds(pl.multiple_of(c * rows, 16), rows)]
    main = []
    for k in range(1, chans):
        d = lax.rem(c + k, chans)
        part = gated.at[:, pl.ds(pl.multiple_of(d * width, width), width)]
        main.append(remote(part, place, ssem.at[k], rsem.at[k], {"chan": d}))
    mine = gated.at[:, pl.ds(pl.multiple_of(c * width, width), width)]
    local = pltpu.make_async_copy(mine, place, lsem)
    side = [
        remote(q.at[pl.ds(own - TAIL, TAIL)], qprev, hs.at[0], hr.at[0], up),
        remote(q.at[pl.ds(0, GROW)], qnext, hs.at[1], hr.at[1], down),
    ]
    for cp in main + [local] + side:
        cp.start()
    for cp in main:
        cp.wait_recv()
    local.wait()
    late = [
        remote(gown.at[pl.ds(own - MEDIUM, MEDIUM)], gprev, hs.at[2], hr.at[2], up),
        remote(gown.at[pl.ds(0, TAIL)], gnext, hs.at[3], hr.at[3], down),
    ]
    for cp in late:
        cp.start()
    for cp in main:
        cp.wait_send()
    for cp in side + late:
        cp.wait()


def third_kernel(chans, seqs, g, out, ssem, rsem, lsem):
    c, _ = spot()
    rows = out.shape[1]
    width = g.shape[2]
    greet(chans, seqs, False, False)
    place = out.at[:, :, pl.ds(pl.multiple_of(c * width, width), width)]

    def part(d):
        return g.at[:, pl.ds(pl.multiple_of(d * (rows - EDGE), 8), rows), :]

    copies = []
    for k in range(1, chans):
        d = lax.rem(c + k, chans)
        copies.append(remote(part(d), place, ssem.at[k], rsem.at[k], {"chan": d}))
    copies.append(pltpu.make_async_copy(part(c), place, lsem))
    for cp in copies:
        cp.start()
    for cp in copies:
        cp.wait()


def open_taps(fm, seg_col, lo, n):
    for j in range(1, SHORT):
        same = seg_col[pl.ds(lo, n), :] == seg_col[pl.ds(lo - j, n), :]
        fm[j - 1, pl.ds(0, n), :] = jnp.where(same, 1.0, 0.0)


def gate_kernel(x, xprev, xnext, taps, seg_col, gated, kv, fm, xs):
    rows = x.shape[1]
    more = rows + EDGE

    @pl.when(pl.program_id(0) == 0)
    def _():
        open_taps(fm, seg_col, EDGE, more)

    f32 = jnp.float32
    for m in range(2):
        xs[m, pl.ds(0, EDGE), :] = xprev[m].astype(f32)
        xs[m, pl.ds(EDGE, rows), :] = x[m + 1].astype(f32)
        xs[m, pl.ds(EDGE + rows, EDGE), :] = xnext[m].astype(f32)
    for t in range(x.shape[2] // LANES):
        at = pl.ds(t * LANES, LANES)
        outs = []
        for m in range(2):
            total = taps[m + 1, 0:1, at] * xs[m, pl.ds(EDGE, more), at]
            for j in range(1, SHORT):
                total = total + taps[m + 1, j : j + 1, at] * (
                    fm[j - 1] * xs[m, pl.ds(EDGE - j, more), at])
            kv[m, :, at] = total
            outs.append(total[:rows])
        gated[:, at] = (outs[0] * outs[1]).astype(jnp.bfloat16)


def last_kernel(g, kv, taps, seg_col, out, fm, gs):
    rows = out.shape[1]
    more = rows + EDGE

    @pl.when(pl.program_id(0) == 0)
    def _():
        open_taps(fm, seg_col, EDGE, more)

    f32 = jnp.float32
    gs[0] = g[0].astype(f32)
    back = g[1].astype(f32)
    gs[1] = back * kv[1]
    gs[2] = back * kv[0]
    for t in range(out.shape[2] // LANES):
        at = pl.ds(t * LANES, LANES)
        for m in range(3):
            total = taps[m, 0:1, at] * gs[m, pl.ds(0, rows), at]
            for j in range(1, SHORT):
                total = total + taps[m, j : j + 1, at] * (
                    fm[j - 1, pl.ds(j, rows), :] * gs[m, pl.ds(j, rows), at])
            out[m, :, at] = total.astype(jnp.bfloat16)


def mix_kernel(own, q, qprev, qnext, gown, gprev, gnext, cot, cnext, taps, filt, filt_rev, seg_col, seg_row,
               hy, grads, xs, fm, mf, mb, lf, lt, gat, gl, sh, cs):
    blocks = own // MEDIUM
    sizes = [MEDIUM] * blocks + [TAIL]
    grow = own + GROW
    f32 = jnp.float32

    @pl.when(pl.program_id(0) == 0)
    def _():
        open_taps(fm, seg_col, TAIL, grow)
        for b, rows in enumerate(sizes):
            r = lax.broadcasted_iota(jnp.int32, (rows, 2 * MEDIUM), 0)
            k = lax.broadcasted_iota(jnp.int32, (rows, 2 * MEDIUM), 1)
            here = jnp.tile(seg_col[pl.ds(TAIL + MEDIUM * b, rows), :], (1, 2))
            past = jnp.broadcast_to(seg_row[0:1, pl.ds(MEDIUM * b, 2 * MEDIUM)], (rows, 2 * MEDIUM))
            lag = r + MEDIUM - k
            ok = (lag >= 0) & (lag < MEDIUM) & (here == past)
            mf[b, pl.ds(0, rows), :] = jnp.where(ok, 1.0, 0.0).astype(jnp.bfloat16)
            ahead = jnp.broadcast_to(seg_row[0:1, pl.ds(MEDIUM * (b + 1), 2 * MEDIUM)], (rows, 2 * MEDIUM))
            lag = k - r
            ok = (lag >= 0) & (lag < MEDIUM) & (here == ahead)
            mb[b, pl.ds(0, rows), :] = jnp.where(ok, 1.0, 0.0).astype(jnp.bfloat16)
        gat[...] = jnp.zeros_like(gat)
        gl[...] = jnp.zeros_like(gl)

    xs[pl.ds(0, TAIL), :] = qprev[...].astype(f32)
    xs[pl.ds(TAIL, own), :] = q[...].astype(f32)
    xs[pl.ds(TAIL + own, GROW), :] = qnext[...].astype(f32)
    cs[pl.ds(0, own), :] = cot[...].astype(f32)
    cs[pl.ds(own, GROW), :] = cnext[...].astype(f32)
    gat[pl.ds(0, MEDIUM), :] = gprev[...]
    gat[pl.ds(MEDIUM, own), :] = gown[...]
    gat[pl.ds(MEDIUM + own, TAIL), :] = gnext[...]
    coef = [taps[0, j : j + 1, :] for j in range(SHORT)]
    step = 80
    for at in range(0, grow, step):
        total = coef[0] * xs[pl.ds(TAIL + at, step), :]
        for j in range(1, SHORT):
            total = total + coef[j] * (fm[j - 1, pl.ds(at, step), :] * xs[pl.ds(TAIL + at - j, step), :])
        if at < own:
            n = min(step, own - at)
            sh[pl.ds(at, n), :] = total[:n]
        gl[pl.ds(at, step), :] = (cs[pl.ds(at, step), :] * total).astype(jnp.bfloat16)

    lane_group = lax.broadcasted_iota(jnp.int32, (MEDIUM, LANES), 1) // (LANES // 8)

    def band(filters, masks):
        for g in range(8):
            row = jnp.broadcast_to(filters[g : g + 1, :], (MEDIUM, MEDIUM))
            circ = pltpu.roll(row, 0, 1, stride=1, stride_axis=0).astype(jnp.bfloat16)
            two = jnp.concatenate([circ, circ], axis=1)
            for b in range(blocks):
                lf[b, pl.ds(g * MEDIUM, MEDIUM), :] = two * masks[b]
            lt[pl.ds(g * TAIL, TAIL), :] = two[:TAIL] * masks[blocks, pl.ds(0, TAIL), :]

    def product(b, source):
        rhs = source[pl.ds(MEDIUM * b, 2 * MEDIUM), :]
        rows = sizes[b]
        lhs = lf[b] if b < blocks else lt[...]
        res = jnp.dot(lhs, rhs, preferred_element_type=f32)
        total = res[:rows]
        for g in range(1, 8):
            total = jnp.where(lane_group[:rows] == g, res[g * rows : (g + 1) * rows], total)
        return total

    band(filt_rev, mf)
    for b, rows in enumerate(sizes):
        long = product(b, gat)
        at = pl.ds(MEDIUM * b, rows)
        if b < blocks:
            hy[at, :] = (sh[at, :] * long).astype(jnp.bfloat16)
        grads[0, at, :] = (cs[at, :] * long).astype(jnp.bfloat16)
    band(filt, mb)
    for b, rows in enumerate(sizes):
        grads[1, pl.ds(MEDIUM * b, rows), :] = product(b, gl).astype(jnp.bfloat16)


def solution(mesh):
    chans, seqs = mesh.shape["chan"], mesh.shape["seq"]

    def body(features, cotangent, short_filter, medium_filter, doc_start):
        own, width = cotangent.shape
        rows, _, full = features.shape
        groups = medium_filter.shape[0]
        span = full // (groups * chans)
        grow = own + GROW
        more = rows + EDGE
        bf, f32 = jnp.bfloat16, jnp.float32
        shape = jax.ShapeDtypeStruct
        dma = pltpu.SemaphoreType.DMA
        x = jnp.transpose(features, (1, 0, 2))
        ctaps = jnp.pad(jnp.transpose(short_filter, (0, 2, 1)), ((0, 0), (0, 1), (0, 0)))
        q, xprev, xnext, taps, cnext = pl.pallas_call(
            functools.partial(first_kernel, chans, seqs),
            out_shape=(
                shape((own, width), bf), shape((2, EDGE, full), bf), shape((2, EDGE, full), bf),
                shape((chans, 3, 8, groups), f32), shape((GROW, width), bf)),
            in_specs=[ANY] * 3,
            out_specs=(ANY,) * 5,
            scratch_shapes=[dma((chans,))] * 4 + [dma((3,)), dma((3,)), dma((2,))],
            compiler_params=pltpu.CompilerParams(collective_id=0, has_side_effects=True),
            name="first_parts",
        )(x, cotangent, ctaps)
        taps = jnp.repeat(jnp.transpose(taps, (1, 2, 0, 3)).reshape(3, 8, groups * chans), span, axis=2)
        mytaps = jnp.repeat(ctaps[:1], span, axis=2)

        tokens = own * seqs
        bounds = jnp.arange(doc_start.shape[0], dtype=jnp.int32) * own + doc_start

        def ids(base, n):
            pos = base + jnp.arange(n, dtype=jnp.int32)
            seg = jnp.sum((bounds[None, :] <= pos[:, None]).astype(jnp.int32), axis=1)
            return jnp.where(pos < 0, -1, jnp.where(pos >= tokens, FAR, seg))

        start = lax.axis_index("seq") * own
        seg = ids(start - MEDIUM, own + 3 * MEDIUM)
        cols = TAIL + grow
        seg_col = jnp.broadcast_to(seg[MEDIUM - TAIL : MEDIUM - TAIL + cols, None], (cols, LANES))
        seg_row = jnp.broadcast_to(seg[None], (8, seg.shape[0]))
        rseg = ids(start + lax.axis_index("chan") * rows - EDGE, rows + 2 * EDGE)
        rseg_col = jnp.broadcast_to(rseg[:, None], (rseg.shape[0], LANES))
        filt = medium_filter.astype(bf).astype(f32)
        filt_rev = jnp.roll(filt[:, ::-1], 1, axis=1)

        whole = lambda dims: pl.BlockSpec(dims, lambda i: (0,) * len(dims))
        flat = lambda n, w: pl.BlockSpec((n, w), lambda i: (0, i))
        cube = lambda m, n, w: pl.BlockSpec((m, n, w), lambda i: (0, 0, i))
        gated, kv = pl.pallas_call(
            gate_kernel,
            grid=(full // WIDE,),
            out_shape=(shape((rows, full), bf), shape((2, more, full), f32)),
            in_specs=[cube(3, rows, WIDE), cube(2, EDGE, WIDE), cube(2, EDGE, WIDE), cube(3, 8, WIDE),
                      whole(rseg_col.shape)],
            out_specs=(flat(rows, WIDE), cube(2, more, WIDE)),
            scratch_shapes=[pltpu.VMEM((SHORT - 1, more, LANES), f32),
                            pltpu.VMEM((2, rows + 2 * EDGE, WIDE), f32)],
            compiler_params=pltpu.CompilerParams(vmem_limit_bytes=40 << 20),
            name="gate_rows",
        )(x, xprev, xnext, taps, rseg_col)

        gown, gprev, gnext, qprev, qnext = pl.pallas_call(
            functools.partial(second_kernel, chans, seqs),
            out_shape=tuple(shape((n, width), bf) for n in (own, MEDIUM, TAIL, TAIL, GROW)),
            in_specs=[ANY] * 2,
            out_specs=(ANY,) * 5,
            scratch_shapes=[dma((chans,))] * 2 + [dma((4,)), dma((4,)), dma],
            compiler_params=pltpu.CompilerParams(collective_id=1, has_side_effects=True),
            name="second_parts",
        )(q, gated)

        blocks = own // MEDIUM
        hy, grads = pl.pallas_call(
            functools.partial(mix_kernel, own),
            grid=(width // LANES,),
            out_shape=(shape((own, width), bf), shape((2, own + TAIL, width), bf)),
            in_specs=[
                flat(own, LANES), flat(TAIL, LANES), flat(GROW, LANES),
                flat(own, LANES), flat(MEDIUM, LANES), flat(TAIL, LANES),
                flat(own, LANES), flat(GROW, LANES),
                cube(1, 8, LANES),
                pl.BlockSpec((8, MEDIUM), lambda i: (i, 0)),
                pl.BlockSpec((8, MEDIUM), lambda i: (i, 0)),
                whole(seg_col.shape), whole(seg_row.shape),
            ],
            out_specs=(flat(own, LANES), cube(2, own + TAIL, LANES)),
            scratch_shapes=[
                pltpu.VMEM((cols, LANES), f32),
                pltpu.VMEM((SHORT - 1, grow, LANES), f32),
                pltpu.VMEM((blocks + 1, MEDIUM, 2 * MEDIUM), bf),
                pltpu.VMEM((blocks + 1, MEDIUM, 2 * MEDIUM), bf),
                pltpu.VMEM((blocks, 8 * MEDIUM, 2 * MEDIUM), bf),
                pltpu.VMEM((8 * TAIL, 2 * MEDIUM), bf),
                pltpu.VMEM((own + 2 * MEDIUM, LANES), bf),
                pltpu.VMEM((own + 2 * MEDIUM, LANES), bf),
                pltpu.VMEM((own, LANES), f32),
                pltpu.VMEM((grow, LANES), f32),
            ],
            compiler_params=pltpu.CompilerParams(vmem_limit_bytes=40 << 20),
            name="mix_tile",
        )(q, qprev, qnext, gown, gprev, gnext, cotangent, cnext, mytaps, filt, filt_rev, seg_col, seg_row)

        back = pl.pallas_call(
            functools.partial(third_kernel, chans, seqs),
            out_shape=shape((2, more, full), bf),
            in_specs=[ANY],
            out_specs=ANY,
            scratch_shapes=[dma((chans,)), dma((chans,)), dma],
            compiler_params=pltpu.CompilerParams(collective_id=2, has_side_effects=True),
            name="third_parts",
        )(grads)

        grad = pl.pallas_call(
            last_kernel,
            grid=(full // WIDE,),
            out_shape=shape((3, rows, full), bf),
            in_specs=[cube(2, more, WIDE), cube(2, more, WIDE), cube(3, 8, WIDE), whole(rseg_col.shape)],
            out_specs=cube(3, rows, WIDE),
            scratch_shapes=[pltpu.VMEM((SHORT - 1, more, LANES), f32), pltpu.VMEM((3, more, WIDE), f32)],
            compiler_params=pltpu.CompilerParams(vmem_limit_bytes=40 << 20),
            name="last_rows",
        )(back, kv, taps, rseg_col)
        return hy, jnp.transpose(grad, (1, 0, 2))

    in_specs = (
        P(("seq", "chan"), None, None),
        P("seq", "chan"),
        P(None, "chan", None),
        P("chan", None),
        P(),
    )
    out_specs = (P("seq", "chan"), P(("seq", "chan"), None, None))
    return jax.shard_map(body, mesh=mesh, in_specs=in_specs, out_specs=out_specs, check_vma=False)
```

```python
import functools

import jax
import jax.numpy as jnp
from jax import lax
from jax.experimental import pallas as pl
from jax.experimental.pallas import tpu as pltpu
from jax.sharding import PartitionSpec as P

SHORT = 7
MEDIUM = 128
EDGE = 8
TAIL = 16
GROW = MEDIUM + TAIL
LANES = 128
WIDE = 1024
FAR = 1 << 20
MESH = pl.DeviceIdType.MESH
ANY = pl.BlockSpec(memory_space=pl.ANY)


def spot():
    return lax.axis_index("chan"), lax.axis_index("seq")


def greet(chans, seqs, ring, line):
    c, s = spot()
    bar = pltpu.get_barrier_semaphore()
    for k in range(1, chans):
        pl.semaphore_signal(bar, inc=1, device_id={"chan": lax.rem(c + k, chans)}, device_id_type=MESH)
    count = chans - 1
    if ring:
        for k in (1, seqs - 1):
            pl.semaphore_signal(bar, inc=1, device_id={"seq": lax.rem(s + k, seqs)}, device_id_type=MESH)
        count += 2
    if line:
        for dev in line_ends(chans, seqs):
            pl.semaphore_signal(bar, inc=1, device_id=dev, device_id_type=MESH)
        count += 2
    pl.semaphore_wait(bar, count)


def line_ends(chans, seqs):
    c, s = spot()
    after = {"seq": lax.rem(s + (c + 1) // chans, seqs), "chan": lax.rem(c + 1, chans)}
    ahead = {"seq": lax.rem(s + seqs - 1 + (c + chans - 1) // chans, seqs), "chan": lax.rem(c + chans - 1, chans)}
    return after, ahead


def remote(src, dst, ssem, rsem, dev):
    return pltpu.make_async_remote_copy(src, dst, ssem, rsem, device_id=dev, device_id_type=MESH)


def first_kernel(chans, seqs, x, cot, ctaps, q, xprev, xnext, taps, cnext, ssem, rsem, tsem, usem, hs, hr, lsem):
    c, s = spot()
    rows = x.shape[1]
    width = q.shape[1]
    greet(chans, seqs, True, True)
    after, ahead = line_ends(chans, seqs)
    copies = [
        remote(x.at[pl.ds(1, 2), pl.ds(rows - EDGE, EDGE)], xprev, hs.at[0], hr.at[0], after),
        remote(x.at[pl.ds(1, 2), pl.ds(0, EDGE)], xnext, hs.at[1], hr.at[1], ahead),
        remote(cot.at[pl.ds(0, GROW)], cnext, hs.at[2], hr.at[2], {"seq": lax.rem(s + seqs - 1, seqs)}),
    ]
    for k in range(1, chans):
        d = lax.rem(c + k, chans)
        copies.append(remote(ctaps, taps.at[c], tsem.at[k], usem.at[k], {"chan": d}))
    place = q.at[pl.ds(pl.multiple_of(c * rows, 16), rows)]
    for k in range(1, chans):
        d = lax.rem(c + k, chans)
        part = x.at[0, :, pl.ds(pl.multiple_of(d * width, width), width)]
        copies.append(remote(part, place, ssem.at[k], rsem.at[k], {"chan": d}))
    mine = x.at[0, :, pl.ds(pl.multiple_of(c * width, width), width)]
    copies.append(pltpu.make_async_copy(mine, place, lsem.at[0]))
    copies.append(pltpu.make_async_copy(ctaps, taps.at[c], lsem.at[1]))
    for cp in copies:
        cp.start()
    for cp in copies:
        cp.wait()


def second_kernel(chans, seqs, q, gated, gown, gprev, gnext, qprev, qnext, ssem, rsem, hs, hr, lsem):
    c, s = spot()
    rows = gated.shape[0]
    own, width = q.shape
    greet(chans, seqs, True, False)
    up, down = {"seq": lax.rem(s + 1, seqs)}, {"seq": lax.rem(s + seqs - 1, seqs)}
    place = gown.at[pl.ds(pl.multiple_of(c * rows, 16), rows)]
    main = []
    for k in range(1, chans):
        d = lax.rem(c + k, chans)
        part = gated.at[:, pl.ds(pl.multiple_of(d * width, width), width)]
        main.append(remote(part, place, ssem.at[k], rsem.at[k], {"chan": d}))
    mine = gated.at[:, pl.ds(pl.multiple_of(c * width, width), width)]
    local = pltpu.make_async_copy(mine, place, lsem)
    side = [
        remote(q.at[pl.ds(own - TAIL, TAIL)], qprev, hs.at[0], hr.at[0], up),
        remote(q.at[pl.ds(0, GROW)], qnext, hs.at[1], hr.at[1], down),
    ]
    for cp in main + [local] + side:
        cp.start()
    for cp in main:
        cp.wait_recv()
    local.wait()
    late = [
        remote(gown.at[pl.ds(own - MEDIUM, MEDIUM)], gprev, hs.at[2], hr.at[2], up),
        remote(gown.at[pl.ds(0, TAIL)], gnext, hs.at[3], hr.at[3], down),
    ]
    for cp in late:
        cp.start()
    for cp in main:
        cp.wait_send()
    for cp in side + late:
        cp.wait()


def expand(t, first, lanes, span):
    bf, f32 = jnp.bfloat16, jnp.float32
    groups = t.shape[1]
    row = lax.broadcasted_iota(jnp.int32, (groups, lanes), 0)
    col = lax.broadcasted_iota(jnp.int32, (groups, lanes), 1)
    hot = jnp.where(row == first + col // span, 1.0, 0.0).astype(bf)
    high = t.astype(bf)
    rest = t - high.astype(f32)
    mid = rest.astype(bf)
    low = (rest - mid.astype(f32)).astype(bf)
    dot = lambda part: jnp.dot(part, hot, preferred_element_type=f32)
    return dot(high) + (dot(mid) + dot(low))


def spread(taps, out, span):
    chans, _, _, groups = taps.shape
    lanes = out.shape[2]
    per = groups * span // lanes
    i = pl.program_id(0)
    full = taps[i // per].reshape(24, groups)
    out[...] = expand(full, lax.rem(i, per) * (lanes // span), lanes, span).reshape(3, 8, lanes)


def open_taps(fm, seg_col, lo, n):
    for j in range(1, SHORT):
        same = seg_col[pl.ds(lo, n), :] == seg_col[pl.ds(lo - j, n), :]
        fm[j - 1, pl.ds(0, n), :] = jnp.where(same, 1.0, 0.0)


def gate_kernel(span, x, xprev, xnext, ctaps, seg_col, gated, kv, fm, xs, taps):
    spread(ctaps, taps, span)
    rows = x.shape[1]
    more = rows + EDGE

    @pl.when(pl.program_id(0) == 0)
    def _():
        open_taps(fm, seg_col, EDGE, more)

    f32 = jnp.float32
    for m in range(2):
        xs[m, pl.ds(0, EDGE), :] = xprev[m].astype(f32)
        xs[m, pl.ds(EDGE, rows), :] = x[m + 1].astype(f32)
        xs[m, pl.ds(EDGE + rows, EDGE), :] = xnext[m].astype(f32)
    for t in range(x.shape[2] // LANES):
        at = pl.ds(t * LANES, LANES)
        outs = []
        for m in range(2):
            total = taps[m + 1, 0:1, at] * xs[m, pl.ds(EDGE, more), at]
            for j in range(1, SHORT):
                total = total + taps[m + 1, j : j + 1, at] * (
                    fm[j - 1] * xs[m, pl.ds(EDGE - j, more), at])
            kv[m, :, at] = total
            outs.append(total[:rows])
        gated[:, at] = (outs[0] * outs[1]).astype(jnp.bfloat16)


def last_kernel(span, g, kv, ctaps, seg_col, out, fm, gs, taps):
    spread(ctaps, taps, span)
    rows = out.shape[1]
    more = rows + EDGE

    @pl.when(pl.program_id(0) == 0)
    def _():
        open_taps(fm, seg_col, EDGE, more)

    f32 = jnp.float32
    gs[0] = g[0].astype(f32)
    back = g[1].astype(f32)
    gs[1] = back * kv[1]
    gs[2] = back * kv[0]
    for t in range(out.shape[2] // LANES):
        at = pl.ds(t * LANES, LANES)
        for m in range(3):
            total = taps[m, 0:1, at] * gs[m, pl.ds(0, rows), at]
            for j in range(1, SHORT):
                total = total + taps[m, j : j + 1, at] * (
                    fm[j - 1, pl.ds(j, rows), :] * gs[m, pl.ds(j, rows), at])
            out[m, :, at] = total.astype(jnp.bfloat16)


def mix_kernel(chans, own, span, q, qprev, qnext, gown, gprev, gnext, cot, cnext, ctaps, filt, filt_rev, seg_col,
               seg_row, hy, out, xs, fm, mf, mb, lf, lt, gat, gl, sh, cs, sent, ssem, rsem, lsem):
    tile = pl.program_id(0)
    c, _ = spot()
    more = out.shape[1]
    rows_dev = more - EDGE
    width = out.shape[2] // chans
    grads = sent.at[tile]
    blocks = own // MEDIUM
    sizes = [MEDIUM] * blocks + [TAIL]
    grow = own + GROW
    f32 = jnp.float32

    def sends(t):
        place = out.at[:, :, pl.ds(pl.multiple_of(c * width + t * LANES, LANES), LANES)]
        part = lambda d: sent.at[t, :, pl.ds(pl.multiple_of(d * rows_dev, 8), more), :]
        made = []
        for k in range(1, chans):
            d = lax.rem(c + k, chans)
            made.append(remote(part(d), place, ssem.at[t, k], rsem.at[t, k], {"chan": d}))
        made.append(pltpu.make_async_copy(part(c), place, lsem.at[t]))
        return made

    @pl.when(tile == 0)
    def _():
        greet(chans, 0, False, False)
        open_taps(fm, seg_col, TAIL, grow)
        for b, rows in enumerate(sizes):
            r = lax.broadcasted_iota(jnp.int32, (rows, 2 * MEDIUM), 0)
            k = lax.broadcasted_iota(jnp.int32, (rows, 2 * MEDIUM), 1)
            here = jnp.tile(seg_col[pl.ds(TAIL + MEDIUM * b, rows), :], (1, 2))
            past = jnp.broadcast_to(seg_row[0:1, pl.ds(MEDIUM * b, 2 * MEDIUM)], (rows, 2 * MEDIUM))
            lag = r + MEDIUM - k
            ok = (lag >= 0) & (lag < MEDIUM) & (here == past)
            mf[b, pl.ds(0, rows), :] = jnp.where(ok, 1.0, 0.0).astype(jnp.bfloat16)
            ahead = jnp.broadcast_to(seg_row[0:1, pl.ds(MEDIUM * (b + 1), 2 * MEDIUM)], (rows, 2 * MEDIUM))
            lag = k - r
            ok = (lag >= 0) & (lag < MEDIUM) & (here == ahead)
            mb[b, pl.ds(0, rows), :] = jnp.where(ok, 1.0, 0.0).astype(jnp.bfloat16)
        gat[...] = jnp.zeros_like(gat)
        gl[...] = jnp.zeros_like(gl)

    xs[pl.ds(0, TAIL), :] = qprev[...].astype(f32)
    xs[pl.ds(TAIL, own), :] = q[...].astype(f32)
    xs[pl.ds(TAIL + own, GROW), :] = qnext[...].astype(f32)
    cs[pl.ds(0, own), :] = cot[...].astype(f32)
    cs[pl.ds(own, GROW), :] = cnext[...].astype(f32)
    gat[pl.ds(0, MEDIUM), :] = gprev[...]
    gat[pl.ds(MEDIUM, own), :] = gown[...]
    gat[pl.ds(MEDIUM + own, TAIL), :] = gnext[...]
    taps = expand(ctaps[0], tile * (LANES // span), LANES, span)
    coef = [taps[j : j + 1, :] for j in range(SHORT)]
    step = 80
    for at in range(0, grow, step):
        total = coef[0] * xs[pl.ds(TAIL + at, step), :]
        for j in range(1, SHORT):
            total = total + coef[j] * (fm[j - 1, pl.ds(at, step), :] * xs[pl.ds(TAIL + at - j, step), :])
        if at < own:
            n = min(step, own - at)
            sh[pl.ds(at, n), :] = total[:n]
        gl[pl.ds(at, step), :] = (cs[pl.ds(at, step), :] * total).astype(jnp.bfloat16)

    lane_group = lax.broadcasted_iota(jnp.int32, (MEDIUM, LANES), 1) // (LANES // 8)

    def band(filters, masks):
        for g in range(8):
            row = jnp.broadcast_to(filters[g : g + 1, :], (MEDIUM, MEDIUM))
            circ = pltpu.roll(row, 0, 1, stride=1, stride_axis=0).astype(jnp.bfloat16)
            two = jnp.concatenate([circ, circ], axis=1)
            for b in range(blocks):
                lf[b, pl.ds(g * MEDIUM, MEDIUM), :] = two * masks[b]
            lt[pl.ds(g * TAIL, TAIL), :] = two[:TAIL] * masks[blocks, pl.ds(0, TAIL), :]

    def product(b, source):
        rhs = source[pl.ds(MEDIUM * b, 2 * MEDIUM), :]
        rows = sizes[b]
        lhs = lf[b] if b < blocks else lt[...]
        res = jnp.dot(lhs, rhs, preferred_element_type=f32)
        total = res[:rows]
        for g in range(1, 8):
            total = jnp.where(lane_group[:rows] == g, res[g * rows : (g + 1) * rows], total)
        return total

    band(filt_rev, mf)
    for b, rows in enumerate(sizes):
        long = product(b, gat)
        at = pl.ds(MEDIUM * b, rows)
        if b < blocks:
            hy[at, :] = (sh[at, :] * long).astype(jnp.bfloat16)
        grads[0, at, :] = (cs[at, :] * long).astype(jnp.bfloat16)
    band(filt, mb)
    for b, rows in enumerate(sizes):
        grads[1, pl.ds(MEDIUM * b, rows), :] = product(b, gl).astype(jnp.bfloat16)

    for cp in sends(tile):
        cp.start()

    @pl.when(tile == pl.num_programs(0) - 1)
    def _():
        def finish(t, carry):
            for cp in sends(t):
                cp.wait()
            return carry

        lax.fori_loop(0, pl.num_programs(0), finish, 0)


def solution(mesh):
    chans, seqs = mesh.shape["chan"], mesh.shape["seq"]

    def body(features, cotangent, short_filter, medium_filter, doc_start):
        own, width = cotangent.shape
        rows, _, full = features.shape
        groups = medium_filter.shape[0]
        span = full // (groups * chans)
        grow = own + GROW
        more = rows + EDGE
        bf, f32 = jnp.bfloat16, jnp.float32
        shape = jax.ShapeDtypeStruct
        dma = pltpu.SemaphoreType.DMA
        x = jnp.transpose(features, (1, 0, 2))
        ctaps = jnp.pad(jnp.transpose(short_filter, (0, 2, 1)), ((0, 0), (0, 1), (0, 0)))
        q, xprev, xnext, taps, cnext = pl.pallas_call(
            functools.partial(first_kernel, chans, seqs),
            out_shape=(
                shape((own, width), bf), shape((2, EDGE, full), bf), shape((2, EDGE, full), bf),
                shape((chans, 3, 8, groups), f32), shape((GROW, width), bf)),
            in_specs=[ANY] * 3,
            out_specs=(ANY,) * 5,
            scratch_shapes=[dma((chans,))] * 4 + [dma((3,)), dma((3,)), dma((2,))],
            compiler_params=pltpu.CompilerParams(collective_id=0, has_side_effects=True, vmem_limit_bytes=60 << 20),
            name="first_parts",
        )(x, cotangent, ctaps)
        wide = min(WIDE, width)
        limit = 60 << 20

        tokens = own * seqs
        bounds = jnp.arange(doc_start.shape[0], dtype=jnp.int32) * own + doc_start

        def ids(base, n):
            pos = base + jnp.arange(n, dtype=jnp.int32)
            seg = jnp.sum((bounds[None, :] <= pos[:, None]).astype(jnp.int32), axis=1)
            return jnp.where(pos < 0, -1, jnp.where(pos >= tokens, FAR, seg))

        start = lax.axis_index("seq") * own
        seg = ids(start - MEDIUM, own + 3 * MEDIUM)
        cols = TAIL + grow
        seg_col = jnp.broadcast_to(seg[MEDIUM - TAIL : MEDIUM - TAIL + cols, None], (cols, LANES))
        seg_row = jnp.broadcast_to(seg[None], (8, seg.shape[0]))
        rseg = ids(start + lax.axis_index("chan") * rows - EDGE, rows + 2 * EDGE)
        rseg_col = jnp.broadcast_to(rseg[:, None], (rseg.shape[0], LANES))
        filt = medium_filter.astype(bf).astype(f32)
        filt_rev = jnp.roll(filt[:, ::-1], 1, axis=1)

        whole = lambda dims: pl.BlockSpec(dims, lambda i: (0,) * len(dims))
        flat = lambda n, w: pl.BlockSpec((n, w), lambda i: (0, i))
        cube = lambda m, n, w: pl.BlockSpec((m, n, w), lambda i: (0, 0, i))
        gated, kv = pl.pallas_call(
            functools.partial(gate_kernel, span),
            grid=(full // wide,),
            out_shape=(shape((rows, full), bf), shape((2, more, full), f32)),
            in_specs=[cube(3, rows, wide), cube(2, EDGE, wide), cube(2, EDGE, wide), whole(taps.shape),
                      whole(rseg_col.shape)],
            out_specs=(flat(rows, wide), cube(2, more, wide)),
            scratch_shapes=[pltpu.VMEM((SHORT - 1, more, LANES), f32),
                            pltpu.VMEM((2, rows + 2 * EDGE, wide), f32), pltpu.VMEM((3, 8, wide), f32)],
            compiler_params=pltpu.CompilerParams(vmem_limit_bytes=limit),
            name="gate_rows",
        )(x, xprev, xnext, taps, rseg_col)

        gown, gprev, gnext, qprev, qnext = pl.pallas_call(
            functools.partial(second_kernel, chans, seqs),
            out_shape=tuple(shape((n, width), bf) for n in (own, MEDIUM, TAIL, TAIL, GROW)),
            in_specs=[ANY] * 2,
            out_specs=(ANY,) * 5,
            scratch_shapes=[dma((chans,))] * 2 + [dma((4,)), dma((4,)), dma],
            compiler_params=pltpu.CompilerParams(collective_id=1, has_side_effects=True, vmem_limit_bytes=limit),
            name="second_parts",
        )(q, gated)

        blocks = own // MEDIUM
        tiles = width // LANES
        hy, back = pl.pallas_call(
            functools.partial(mix_kernel, chans, own, span),
            grid=(width // LANES,),
            out_shape=(shape((own, width), bf), shape((2, more, full), bf)),
            in_specs=[
                flat(own, LANES), flat(TAIL, LANES), flat(GROW, LANES),
                flat(own, LANES), flat(MEDIUM, LANES), flat(TAIL, LANES),
                flat(own, LANES), flat(GROW, LANES),
                whole((1, 8, groups)),
                pl.BlockSpec((8, MEDIUM), lambda i: (i, 0)),
                pl.BlockSpec((8, MEDIUM), lambda i: (i, 0)),
                whole(seg_col.shape), whole(seg_row.shape),
            ],
            out_specs=(flat(own, LANES), ANY),
            scratch_shapes=[
                pltpu.VMEM((cols, LANES), f32),
                pltpu.VMEM((SHORT - 1, grow, LANES), f32),
                pltpu.VMEM((blocks + 1, MEDIUM, 2 * MEDIUM), bf),
                pltpu.VMEM((blocks + 1, MEDIUM, 2 * MEDIUM), bf),
                pltpu.VMEM((blocks, 8 * MEDIUM, 2 * MEDIUM), bf),
                pltpu.VMEM((8 * TAIL, 2 * MEDIUM), bf),
                pltpu.VMEM((own + 2 * MEDIUM, LANES), bf),
                pltpu.VMEM((own + 2 * MEDIUM, LANES), bf),
                pltpu.VMEM((own, LANES), f32),
                pltpu.VMEM((grow, LANES), f32),
                pltpu.VMEM((tiles, 2, own + TAIL, LANES), bf),
                dma((tiles, chans)), dma((tiles, chans)), dma((tiles,)),
            ],
            compiler_params=pltpu.CompilerParams(
                collective_id=2, has_side_effects=True, vmem_limit_bytes=limit),
            name="mix_tile",
        )(q, qprev, qnext, gown, gprev, gnext, cotangent, cnext, ctaps[:1], filt, filt_rev, seg_col, seg_row)

        grad = pl.pallas_call(
            functools.partial(last_kernel, span),
            grid=(full // wide,),
            out_shape=shape((3, rows, full), bf),
            in_specs=[cube(2, more, wide), cube(2, more, wide), whole(taps.shape), whole(rseg_col.shape)],
            out_specs=cube(3, rows, wide),
            scratch_shapes=[pltpu.VMEM((SHORT - 1, more, LANES), f32), pltpu.VMEM((3, more, wide), f32),
                            pltpu.VMEM((3, 8, wide), f32)],
            compiler_params=pltpu.CompilerParams(vmem_limit_bytes=limit),
            name="last_rows",
        )(back, kv, taps, rseg_col)
        return hy, jnp.transpose(grad, (1, 0, 2))

    in_specs = (
        P(("seq", "chan"), None, None),
        P("seq", "chan"),
        P(None, "chan", None),
        P("chan", None),
        P(),
    )
    out_specs = (P("seq", "chan"), P(("seq", "chan"), None, None))
    return jax.shard_map(body, mesh=mesh, in_specs=in_specs, out_specs=out_specs, check_vma=False)
```

```python
import functools

import jax
import jax.numpy as jnp
from jax import lax
from jax.experimental import pallas as pl
from jax.experimental.pallas import tpu as pltpu
from jax.sharding import PartitionSpec as P

SHORT = 7
MEDIUM = 128
EDGE = 8
TAIL = 16
GROW = MEDIUM + TAIL
LANES = 128
WIDE = 1024
FAR = 1 << 20
MESH = pl.DeviceIdType.MESH
ANY = pl.BlockSpec(memory_space=pl.ANY)


def spot():
    return lax.axis_index("chan"), lax.axis_index("seq")


def greet(chans, seqs, ring, line):
    c, s = spot()
    bar = pltpu.get_barrier_semaphore()
    for k in range(1, chans):
        pl.semaphore_signal(bar, inc=1, device_id={"chan": lax.rem(c + k, chans)}, device_id_type=MESH)
    count = chans - 1
    if ring:
        for k in (1, seqs - 1):
            pl.semaphore_signal(bar, inc=1, device_id={"seq": lax.rem(s + k, seqs)}, device_id_type=MESH)
        count += 2
    if line:
        for dev in line_ends(chans, seqs):
            pl.semaphore_signal(bar, inc=1, device_id=dev, device_id_type=MESH)
        count += 2
    pl.semaphore_wait(bar, count)


def line_ends(chans, seqs):
    c, s = spot()
    after = {"seq": lax.rem(s + (c + 1) // chans, seqs), "chan": lax.rem(c + 1, chans)}
    ahead = {"seq": lax.rem(s + seqs - 1 + (c + chans - 1) // chans, seqs), "chan": lax.rem(c + chans - 1, chans)}
    return after, ahead


def remote(src, dst, ssem, rsem, dev):
    return pltpu.make_async_remote_copy(src, dst, ssem, rsem, device_id=dev, device_id_type=MESH)


def front_kernel(chans, seqs, span, wide, x, cot, ctaps, seg_col, q, taps, cnext, gown, gprev, gnext, qprev, qnext, kv,
                 xk, xprev, xnext, gated, kvv, fm, xs, tw, qs, qr, ts, tr, cs, cr, cl, hs, hr, ks, lsem):
    c, s = spot()
    rows = x.shape[1]
    more = rows + EDGE
    own, width = q.shape
    per = width // wide
    half = chans // 2
    f32 = jnp.float32
    greet(chans, seqs, True, True)
    after, ahead = line_ends(chans, seqs)
    up, down = {"seq": lax.rem(s + 1, seqs)}, {"seq": lax.rem(s + seqs - 1, seqs)}
    mine = pl.ds(pl.multiple_of(c * rows, 16), rows)
    early = [
        remote(x.at[pl.ds(1, 2), pl.ds(rows - EDGE, EDGE)], xprev, hs.at[0], hr.at[0], after),
        remote(x.at[pl.ds(1, 2), pl.ds(0, EDGE)], xnext, hs.at[1], hr.at[1], ahead),
        pltpu.make_async_copy(x.at[pl.ds(1, 2)], xk, lsem.at[0]),
        pltpu.make_async_copy(ctaps, taps.at[c], lsem.at[1]),
    ]
    queries = []
    for k in range(1, chans):
        d = lax.rem(c + k, chans)
        early.append(remote(ctaps, taps.at[c], ts.at[k], tr.at[k], {"chan": d}))
        part = x.at[0, :, pl.ds(pl.multiple_of(d * width, width), width)]
        queries.append(remote(part, q.at[mine], qs.at[k], qr.at[k], {"chan": d}))
    part = x.at[0, :, pl.ds(pl.multiple_of(c * width, width), width)]
    qlocal = pltpu.make_async_copy(part, q.at[mine], lsem.at[2])
    side = [remote(cot.at[pl.ds(0, GROW)], cnext, hs.at[2], hr.at[2], down)]
    for cp in early + queries + [qlocal] + side:
        cp.start()
    open_taps(fm, seg_col, EDGE, more)
    for cp in early:
        cp.wait()

    def columns(n):
        d = lax.rem(c + half + n // per, chans)
        i = d * per + lax.rem(n, per)
        return d, i, pl.ds(pl.multiple_of(i * wide, wide), wide)

    def chunk_send(n):
        k, p = n // per, lax.rem(n, per)
        d, _, at = columns(n)
        place = gown.at[mine, pl.ds(pl.multiple_of(p * wide, wide), wide)]
        far = remote(gated.at[:, at], place, cs.at[n], cr.at[n], {"chan": d})
        near = pltpu.make_async_copy(gated.at[:, at], place, cl.at[p])
        return k == chans - half, far, near

    def chunk_keep(n):
        at = columns(n)[2]
        return pltpu.make_async_copy(kvv.at[:, :, at], kv.at[:, :, at], ks.at[n])

    def chunk(n, carry):
        _, i, at = columns(n)
        full = taps[i // per].reshape(24, taps.shape[3])
        tw[...] = expand(full, lax.rem(i, per) * (wide // span), wide, span).reshape(3, 8, wide)
        for m in range(2):
            xs[m, pl.ds(0, EDGE), :] = xprev[m, :, at].astype(f32)
            xs[m, pl.ds(EDGE, rows), :] = xk[m, :, at].astype(f32)
            xs[m, pl.ds(EDGE + rows, EDGE), :] = xnext[m, :, at].astype(f32)
        base = i * wide
        for t in range(wide // LANES):
            lane = pl.ds(t * LANES, LANES)
            to = pl.ds(pl.multiple_of(base + t * LANES, LANES), LANES)
            outs = []
            for m in range(2):
                total = tw[m + 1, 0:1, lane] * xs[m, pl.ds(EDGE, more), lane]
                for j in range(1, SHORT):
                    total = total + tw[m + 1, j : j + 1, lane] * (
                        fm[j - 1] * xs[m, pl.ds(EDGE - j, more), lane])
                kvv[m, :, to] = total
                outs.append(total[:rows])
            gated[:, to] = (outs[0] * outs[1]).astype(jnp.bfloat16)
        home, far, near = chunk_send(n)

        @pl.when(home)
        def _():
            near.start()

        @pl.when(jnp.logical_not(home))
        def _():
            far.start()

        chunk_keep(n).start()
        return carry

    lax.fori_loop(0, chans * per, chunk, 0)
    for cp in queries:
        cp.wait_recv()
    qlocal.wait()
    heads = [
        remote(q.at[pl.ds(own - TAIL, TAIL)], qprev, hs.at[3], hr.at[3], up),
        remote(q.at[pl.ds(0, GROW)], qnext, hs.at[4], hr.at[4], down),
    ]
    for cp in heads:
        cp.start()

    def arrive(n, carry):
        home, far, near = chunk_send(n)

        @pl.when(home)
        def _():
            near.wait()

        @pl.when(jnp.logical_not(home))
        def _():
            far.wait_recv()

        return carry

    lax.fori_loop(0, chans * per, arrive, 0)
    late = [
        remote(gown.at[pl.ds(own - MEDIUM, MEDIUM)], gprev, hs.at[5], hr.at[5], up),
        remote(gown.at[pl.ds(0, TAIL)], gnext, hs.at[6], hr.at[6], down),
    ]
    for cp in late:
        cp.start()

    def leave(n, carry):
        home, far, _ = chunk_send(n)

        @pl.when(jnp.logical_not(home))
        def _():
            far.wait_send()

        chunk_keep(n).wait()
        return carry

    lax.fori_loop(0, chans * per, leave, 0)
    for cp in queries:
        cp.wait_send()
    for cp in side + heads + late:
        cp.wait()


def expand(t, first, lanes, span):
    bf, f32 = jnp.bfloat16, jnp.float32
    groups = t.shape[1]
    row = lax.broadcasted_iota(jnp.int32, (groups, lanes), 0)
    col = lax.broadcasted_iota(jnp.int32, (groups, lanes), 1)
    hot = jnp.where(row == first + col // span, 1.0, 0.0).astype(bf)
    high = t.astype(bf)
    rest = t - high.astype(f32)
    mid = rest.astype(bf)
    low = (rest - mid.astype(f32)).astype(bf)
    dot = lambda part: jnp.dot(part, hot, preferred_element_type=f32)
    return dot(high) + (dot(mid) + dot(low))


def spread(taps, out, span):
    chans, _, _, groups = taps.shape
    lanes = out.shape[2]
    per = groups * span // lanes
    i = pl.program_id(0)
    full = taps[i // per].reshape(24, groups)
    out[...] = expand(full, lax.rem(i, per) * (lanes // span), lanes, span).reshape(3, 8, lanes)


def open_taps(fm, seg_col, lo, n):
    for j in range(1, SHORT):
        same = seg_col[pl.ds(lo, n), :] == seg_col[pl.ds(lo - j, n), :]
        fm[j - 1, pl.ds(0, n), :] = jnp.where(same, 1.0, 0.0)


def last_kernel(span, g, kv, ctaps, seg_col, out, fm, gs, taps):
    spread(ctaps, taps, span)
    rows = out.shape[1]
    more = rows + EDGE

    @pl.when(pl.program_id(0) == 0)
    def _():
        open_taps(fm, seg_col, EDGE, more)

    f32 = jnp.float32
    gs[0] = g[0].astype(f32)
    back = g[1].astype(f32)
    gs[1] = back * kv[1]
    gs[2] = back * kv[0]
    for t in range(out.shape[2] // LANES):
        at = pl.ds(t * LANES, LANES)
        for m in range(3):
            total = taps[m, 0:1, at] * gs[m, pl.ds(0, rows), at]
            for j in range(1, SHORT):
                total = total + taps[m, j : j + 1, at] * (
                    fm[j - 1, pl.ds(j, rows), :] * gs[m, pl.ds(j, rows), at])
            out[m, :, at] = total.astype(jnp.bfloat16)


def mix_kernel(chans, own, span, q, qprev, qnext, gown, gprev, gnext, cot, cnext, ctaps, filt, filt_rev, seg_col,
               seg_row, hy, out, xs, fm, mf, mb, lf, lt, gat, gl, sh, cs, sent, ssem, rsem, lsem):
    tile = pl.program_id(0)
    c, _ = spot()
    more = out.shape[1]
    rows_dev = more - EDGE
    width = out.shape[2] // chans
    grads = sent.at[tile]
    blocks = own // MEDIUM
    sizes = [MEDIUM] * blocks + [TAIL]
    grow = own + GROW
    f32 = jnp.float32

    def sends(t):
        place = out.at[:, :, pl.ds(pl.multiple_of(c * width + t * LANES, LANES), LANES)]
        part = lambda d: sent.at[t, :, pl.ds(pl.multiple_of(d * rows_dev, 8), more), :]
        made = []
        for k in range(1, chans):
            d = lax.rem(c + k, chans)
            made.append(remote(part(d), place, ssem.at[t, k], rsem.at[t, k], {"chan": d}))
        made.append(pltpu.make_async_copy(part(c), place, lsem.at[t]))
        return made

    @pl.when(tile == 0)
    def _():
        greet(chans, 0, False, False)
        open_taps(fm, seg_col, TAIL, grow)
        for b, rows in enumerate(sizes):
            r = lax.broadcasted_iota(jnp.int32, (rows, 2 * MEDIUM), 0)
            k = lax.broadcasted_iota(jnp.int32, (rows, 2 * MEDIUM), 1)
            here = jnp.tile(seg_col[pl.ds(TAIL + MEDIUM * b, rows), :], (1, 2))
            past = jnp.broadcast_to(seg_row[0:1, pl.ds(MEDIUM * b, 2 * MEDIUM)], (rows, 2 * MEDIUM))
            lag = r + MEDIUM - k
            ok = (lag >= 0) & (lag < MEDIUM) & (here == past)
            mf[b, pl.ds(0, rows), :] = jnp.where(ok, 1.0, 0.0).astype(jnp.bfloat16)
            ahead = jnp.broadcast_to(seg_row[0:1, pl.ds(MEDIUM * (b + 1), 2 * MEDIUM)], (rows, 2 * MEDIUM))
            lag = k - r
            ok = (lag >= 0) & (lag < MEDIUM) & (here == ahead)
            mb[b, pl.ds(0, rows), :] = jnp.where(ok, 1.0, 0.0).astype(jnp.bfloat16)
        gat[...] = jnp.zeros_like(gat)
        gl[...] = jnp.zeros_like(gl)

    xs[pl.ds(0, TAIL), :] = qprev[...].astype(f32)
    xs[pl.ds(TAIL, own), :] = q[...].astype(f32)
    xs[pl.ds(TAIL + own, GROW), :] = qnext[...].astype(f32)
    cs[pl.ds(0, own), :] = cot[...].astype(f32)
    cs[pl.ds(own, GROW), :] = cnext[...].astype(f32)
    gat[pl.ds(0, MEDIUM), :] = gprev[...]
    gat[pl.ds(MEDIUM, own), :] = gown[...]
    gat[pl.ds(MEDIUM + own, TAIL), :] = gnext[...]
    taps = expand(ctaps[0], tile * (LANES // span), LANES, span)
    coef = [taps[j : j + 1, :] for j in range(SHORT)]
    step = 80
    for at in range(0, grow, step):
        total = coef[0] * xs[pl.ds(TAIL + at, step), :]
        for j in range(1, SHORT):
            total = total + coef[j] * (fm[j - 1, pl.ds(at, step), :] * xs[pl.ds(TAIL + at - j, step), :])
        if at < own:
            n = min(step, own - at)
            sh[pl.ds(at, n), :] = total[:n]
        gl[pl.ds(at, step), :] = (cs[pl.ds(at, step), :] * total).astype(jnp.bfloat16)

    lane_group = lax.broadcasted_iota(jnp.int32, (MEDIUM, LANES), 1) // (LANES // 8)

    def band(filters, masks):
        for g in range(8):
            row = jnp.broadcast_to(filters[g : g + 1, :], (MEDIUM, MEDIUM))
            circ = pltpu.roll(row, 0, 1, stride=1, stride_axis=0).astype(jnp.bfloat16)
            two = jnp.concatenate([circ, circ], axis=1)
            for b in range(blocks):
                lf[b, pl.ds(g * MEDIUM, MEDIUM), :] = two * masks[b]
            lt[pl.ds(g * TAIL, TAIL), :] = two[:TAIL] * masks[blocks, pl.ds(0, TAIL), :]

    def product(b, source):
        rhs = source[pl.ds(MEDIUM * b, 2 * MEDIUM), :]
        rows = sizes[b]
        lhs = lf[b] if b < blocks else lt[...]
        res = jnp.dot(lhs, rhs, preferred_element_type=f32)
        total = res[:rows]
        for g in range(1, 8):
            total = jnp.where(lane_group[:rows] == g, res[g * rows : (g + 1) * rows], total)
        return total

    band(filt_rev, mf)
    for b, rows in enumerate(sizes):
        long = product(b, gat)
        at = pl.ds(MEDIUM * b, rows)
        if b < blocks:
            hy[at, :] = (sh[at, :] * long).astype(jnp.bfloat16)
        grads[0, at, :] = (cs[at, :] * long).astype(jnp.bfloat16)
    band(filt, mb)
    for b, rows in enumerate(sizes):
        grads[1, pl.ds(MEDIUM * b, rows), :] = product(b, gl).astype(jnp.bfloat16)

    for cp in sends(tile):
        cp.start()

    @pl.when(tile == pl.num_programs(0) - 1)
    def _():
        def finish(t, carry):
            for cp in sends(t):
                cp.wait()
            return carry

        lax.fori_loop(0, pl.num_programs(0), finish, 0)


def solution(mesh):
    chans, seqs = mesh.shape["chan"], mesh.shape["seq"]

    def body(features, cotangent, short_filter, medium_filter, doc_start):
        own, width = cotangent.shape
        rows, _, full = features.shape
        groups = medium_filter.shape[0]
        span = full // (groups * chans)
        grow = own + GROW
        more = rows + EDGE
        bf, f32 = jnp.bfloat16, jnp.float32
        shape = jax.ShapeDtypeStruct
        dma = pltpu.SemaphoreType.DMA
        x = jnp.transpose(features, (1, 0, 2))
        ctaps = jnp.pad(jnp.transpose(short_filter, (0, 2, 1)), ((0, 0), (0, 1), (0, 0)))
        wide = min(WIDE, width)
        limit = 60 << 20

        tokens = own * seqs
        bounds = jnp.arange(doc_start.shape[0], dtype=jnp.int32) * own + doc_start

        def ids(base, n):
            pos = base + jnp.arange(n, dtype=jnp.int32)
            seg = jnp.sum((bounds[None, :] <= pos[:, None]).astype(jnp.int32), axis=1)
            return jnp.where(pos < 0, -1, jnp.where(pos >= tokens, FAR, seg))

        start = lax.axis_index("seq") * own
        seg = ids(start - MEDIUM, own + 3 * MEDIUM)
        cols = TAIL + grow
        seg_col = jnp.broadcast_to(seg[MEDIUM - TAIL : MEDIUM - TAIL + cols, None], (cols, LANES))
        seg_row = jnp.broadcast_to(seg[None], (8, seg.shape[0]))
        rseg = ids(start + lax.axis_index("chan") * rows - EDGE, rows + 2 * EDGE)
        rseg_col = jnp.broadcast_to(rseg[:, None], (rseg.shape[0], LANES))
        filt = medium_filter.astype(bf).astype(f32)
        filt_rev = jnp.roll(filt[:, ::-1], 1, axis=1)

        whole = lambda dims: pl.BlockSpec(dims, lambda i: (0,) * len(dims))
        flat = lambda n, w: pl.BlockSpec((n, w), lambda i: (0, i))
        cube = lambda m, n, w: pl.BlockSpec((m, n, w), lambda i: (0, 0, i))
        pieces = chans * (width // wide)
        vmem = pl.BlockSpec(memory_space=pltpu.VMEM)
        parts = lambda n: shape((n, width), bf)
        q, taps, cnext, gown, gprev, gnext, qprev, qnext, kv = pl.pallas_call(
            functools.partial(front_kernel, chans, seqs, span, wide),
            out_shape=(
                parts(own), shape((chans, 3, 8, groups), f32), parts(GROW), parts(own), parts(MEDIUM), parts(TAIL),
                parts(TAIL), parts(GROW), shape((2, more, full), f32)),
            in_specs=[ANY, ANY, ANY, vmem],
            out_specs=(ANY, vmem) + (ANY,) * 7,
            scratch_shapes=[
                pltpu.VMEM((2, rows, full), bf), pltpu.VMEM((2, EDGE, full), bf), pltpu.VMEM((2, EDGE, full), bf),
                pltpu.VMEM((rows, full), bf), pltpu.VMEM((2, more, full), f32),
                pltpu.VMEM((SHORT - 1, more, LANES), f32), pltpu.VMEM((2, rows + 2 * EDGE, wide), f32),
                pltpu.VMEM((3, 8, wide), f32),
                dma((chans,)), dma((chans,)), dma((chans,)), dma((chans,)),
                dma((pieces,)), dma((pieces,)), dma((width // wide,)),
                dma((7,)), dma((7,)), dma((pieces,)), dma((3,)),
            ],
            compiler_params=pltpu.CompilerParams(
                collective_id=0, has_side_effects=True, vmem_limit_bytes=limit),
            name="front",
        )(x, cotangent, ctaps, rseg_col)

        blocks = own // MEDIUM
        tiles = width // LANES
        hy, back = pl.pallas_call(
            functools.partial(mix_kernel, chans, own, span),
            grid=(width // LANES,),
            out_shape=(shape((own, width), bf), shape((2, more, full), bf)),
            in_specs=[
                flat(own, LANES), flat(TAIL, LANES), flat(GROW, LANES),
                flat(own, LANES), flat(MEDIUM, LANES), flat(TAIL, LANES),
                flat(own, LANES), flat(GROW, LANES),
                whole((1, 8, groups)),
                pl.BlockSpec((8, MEDIUM), lambda i: (i, 0)),
                pl.BlockSpec((8, MEDIUM), lambda i: (i, 0)),
                whole(seg_col.shape), whole(seg_row.shape),
            ],
            out_specs=(flat(own, LANES), ANY),
            scratch_shapes=[
                pltpu.VMEM((cols, LANES), f32),
                pltpu.VMEM((SHORT - 1, grow, LANES), f32),
                pltpu.VMEM((blocks + 1, MEDIUM, 2 * MEDIUM), bf),
                pltpu.VMEM((blocks + 1, MEDIUM, 2 * MEDIUM), bf),
                pltpu.VMEM((blocks, 8 * MEDIUM, 2 * MEDIUM), bf),
                pltpu.VMEM((8 * TAIL, 2 * MEDIUM), bf),
                pltpu.VMEM((own + 2 * MEDIUM, LANES), bf),
                pltpu.VMEM((own + 2 * MEDIUM, LANES), bf),
                pltpu.VMEM((own, LANES), f32),
                pltpu.VMEM((grow, LANES), f32),
                pltpu.VMEM((tiles, 2, own + TAIL, LANES), bf),
                dma((tiles, chans)), dma((tiles, chans)), dma((tiles,)),
            ],
            compiler_params=pltpu.CompilerParams(
                collective_id=2, has_side_effects=True, vmem_limit_bytes=limit),
            name="mix_tile",
        )(q, qprev, qnext, gown, gprev, gnext, cotangent, cnext, ctaps[:1], filt, filt_rev, seg_col, seg_row)

        grad = pl.pallas_call(
            functools.partial(last_kernel, span),
            grid=(full // wide,),
            out_shape=shape((3, rows, full), bf),
            in_specs=[cube(2, more, wide), cube(2, more, wide), whole(taps.shape), whole(rseg_col.shape)],
            out_specs=cube(3, rows, wide),
            scratch_shapes=[pltpu.VMEM((SHORT - 1, more, LANES), f32), pltpu.VMEM((3, more, wide), f32),
                            pltpu.VMEM((3, 8, wide), f32)],
            compiler_params=pltpu.CompilerParams(vmem_limit_bytes=limit),
            name="last_rows",
        )(back, kv, taps, rseg_col)
        return hy, jnp.transpose(grad, (1, 0, 2))

    in_specs = (
        P(("seq", "chan"), None, None),
        P("seq", "chan"),
        P(None, "chan", None),
        P("chan", None),
        P(),
    )
    out_specs = (P("seq", "chan"), P(("seq", "chan"), None, None))
    return jax.shard_map(body, mesh=mesh, in_specs=in_specs, out_specs=out_specs, check_vma=False)
```

```python
import functools

import jax
import jax.numpy as jnp
from jax import lax
from jax.experimental import pallas as pl
from jax.experimental.pallas import tpu as pltpu
from jax.sharding import PartitionSpec as P

SHORT = 7
MEDIUM = 128
EDGE = 8
TAIL = 16
GROW = MEDIUM + TAIL
LANES = 128
WIDE = 1024
FAR = 1 << 20
MESH = pl.DeviceIdType.MESH
ANY = pl.BlockSpec(memory_space=pl.ANY)


def spot():
    return lax.axis_index("chan"), lax.axis_index("seq")


def greet(chans, seqs, ring, line):
    c, s = spot()
    bar = pltpu.get_barrier_semaphore()
    for k in range(1, chans):
        pl.semaphore_signal(bar, inc=1, device_id={"chan": lax.rem(c + k, chans)}, device_id_type=MESH)
    count = chans - 1
    if ring:
        for k in (1, seqs - 1):
            pl.semaphore_signal(bar, inc=1, device_id={"seq": lax.rem(s + k, seqs)}, device_id_type=MESH)
        count += 2
    if line:
        for dev in line_ends(chans, seqs):
            pl.semaphore_signal(bar, inc=1, device_id=dev, device_id_type=MESH)
        count += 2
    pl.semaphore_wait(bar, count)


def line_ends(chans, seqs):
    c, s = spot()
    after = {"seq": lax.rem(s + (c + 1) // chans, seqs), "chan": lax.rem(c + 1, chans)}
    ahead = {"seq": lax.rem(s + seqs - 1 + (c + chans - 1) // chans, seqs), "chan": lax.rem(c + chans - 1, chans)}
    return after, ahead


def remote(src, dst, ssem, rsem, dev):
    return pltpu.make_async_remote_copy(src, dst, ssem, rsem, device_id=dev, device_id_type=MESH)


def front_kernel(chans, seqs, span, wide, x, cot, ctaps, seg_col, q, taps, cnext, gown, gprev, gnext, qprev, qnext, kv,
                 xk, xprev, xnext, gated, kvv, fm, xs, tw, qs, qr, ts, tr, cs, cr, cl, hs, hr, ks, lsem):
    c, s = spot()
    rows = x.shape[1]
    more = rows + EDGE
    own, width = q.shape
    per = width // wide
    half = chans // 2
    f32 = jnp.float32
    greet(chans, seqs, True, True)
    after, ahead = line_ends(chans, seqs)
    up, down = {"seq": lax.rem(s + 1, seqs)}, {"seq": lax.rem(s + seqs - 1, seqs)}
    mine = pl.ds(pl.multiple_of(c * rows, 16), rows)
    early = [
        remote(x.at[pl.ds(1, 2), pl.ds(rows - EDGE, EDGE)], xprev, hs.at[0], hr.at[0], after),
        remote(x.at[pl.ds(1, 2), pl.ds(0, EDGE)], xnext, hs.at[1], hr.at[1], ahead),
        pltpu.make_async_copy(x.at[pl.ds(1, 2)], xk, lsem.at[0]),
        pltpu.make_async_copy(ctaps, taps.at[c], lsem.at[1]),
    ]
    queries = []
    for k in range(1, chans):
        d = lax.rem(c + k, chans)
        early.append(remote(ctaps, taps.at[c], ts.at[k], tr.at[k], {"chan": d}))
        part = x.at[0, :, pl.ds(pl.multiple_of(d * width, width), width)]
        queries.append(remote(part, q.at[mine], qs.at[k], qr.at[k], {"chan": d}))
    part = x.at[0, :, pl.ds(pl.multiple_of(c * width, width), width)]
    qlocal = pltpu.make_async_copy(part, q.at[mine], lsem.at[2])
    side = [remote(cot.at[pl.ds(0, GROW)], cnext, hs.at[2], hr.at[2], down)]
    for cp in early + side:
        cp.start()
    open_taps(fm, seg_col, EDGE, more)
    for cp in early:
        cp.wait()
    for cp in queries + [qlocal]:
        cp.start()

    def columns(n):
        d = lax.rem(c + half + lax.rem(n, chans), chans)
        i = d * per + n // chans
        return d, i, pl.ds(pl.multiple_of(i * wide, wide), wide)

    def chunk_send(n):
        k, p = lax.rem(n, chans), n // chans
        d, _, at = columns(n)
        place = gown.at[mine, pl.ds(pl.multiple_of(p * wide, wide), wide)]
        far = remote(gated.at[:, at], place, cs.at[n], cr.at[n], {"chan": d})
        near = pltpu.make_async_copy(gated.at[:, at], place, cl.at[p])
        return k == chans - half, far, near

    def chunk_keep(n):
        at = columns(n)[2]
        return pltpu.make_async_copy(kvv.at[:, :, at], kv.at[:, :, at], ks.at[n])

    def chunk(n, carry):
        _, i, at = columns(n)
        full = taps[i // per].reshape(24, taps.shape[3])
        tw[...] = expand(full, lax.rem(i, per) * (wide // span), wide, span).reshape(3, 8, wide)
        for m in range(2):
            xs[m, pl.ds(0, EDGE), :] = xprev[m, :, at].astype(f32)
            xs[m, pl.ds(EDGE, rows), :] = xk[m, :, at].astype(f32)
            xs[m, pl.ds(EDGE + rows, EDGE), :] = xnext[m, :, at].astype(f32)
        base = i * wide
        for t in range(wide // LANES):
            lane = pl.ds(t * LANES, LANES)
            to = pl.ds(pl.multiple_of(base + t * LANES, LANES), LANES)
            outs = []
            for m in range(2):
                total = tw[m + 1, 0:1, lane] * xs[m, pl.ds(EDGE, more), lane]
                for j in range(1, SHORT):
                    total = total + tw[m + 1, j : j + 1, lane] * (
                        fm[j - 1] * xs[m, pl.ds(EDGE - j, more), lane])
                kvv[m, :, to] = total
                outs.append(total[:rows])
            gated[:, to] = (outs[0] * outs[1]).astype(jnp.bfloat16)
        home, far, near = chunk_send(n)

        @pl.when(home)
        def _():
            near.start()

        @pl.when(jnp.logical_not(home))
        def _():
            far.start()

        chunk_keep(n).start()
        return carry

    lax.fori_loop(0, chans * per, chunk, 0)
    for cp in queries:
        cp.wait_recv()
    qlocal.wait()
    heads = [
        remote(q.at[pl.ds(own - TAIL, TAIL)], qprev, hs.at[3], hr.at[3], up),
        remote(q.at[pl.ds(0, GROW)], qnext, hs.at[4], hr.at[4], down),
    ]
    for cp in heads:
        cp.start()

    def arrive(n, carry):
        home, far, near = chunk_send(n)

        @pl.when(home)
        def _():
            near.wait()

        @pl.when(jnp.logical_not(home))
        def _():
            far.wait_recv()

        return carry

    late = []
    for p in range(per):
        lax.fori_loop(p * chans, (p + 1) * chans, arrive, 0)
        at, e = pl.ds(p * wide, wide), 5 + 2 * p
        late.append(remote(
            gown.at[pl.ds(own - MEDIUM, MEDIUM), at], gprev.at[:, at], hs.at[e], hr.at[e], up))
        late.append(remote(
            gown.at[pl.ds(0, TAIL), at], gnext.at[:, at], hs.at[e + 1], hr.at[e + 1], down))
        for cp in late[-2:]:
            cp.start()

    def leave(n, carry):
        home, far, _ = chunk_send(n)

        @pl.when(jnp.logical_not(home))
        def _():
            far.wait_send()

        chunk_keep(n).wait()
        return carry

    lax.fori_loop(0, chans * per, leave, 0)
    for cp in queries:
        cp.wait_send()
    for cp in side + heads + late:
        cp.wait()


def expand(t, first, lanes, span):
    bf, f32 = jnp.bfloat16, jnp.float32
    groups = t.shape[1]
    row = lax.broadcasted_iota(jnp.int32, (groups, lanes), 0)
    col = lax.broadcasted_iota(jnp.int32, (groups, lanes), 1)
    hot = jnp.where(row == first + col // span, 1.0, 0.0).astype(bf)
    high = t.astype(bf)
    rest = t - high.astype(f32)
    mid = rest.astype(bf)
    low = (rest - mid.astype(f32)).astype(bf)
    dot = lambda part: jnp.dot(part, hot, preferred_element_type=f32)
    return dot(high) + (dot(mid) + dot(low))


def spread(taps, out, span):
    chans, _, _, groups = taps.shape
    lanes = out.shape[2]
    per = groups * span // lanes
    i = pl.program_id(0)
    full = taps[i // per].reshape(24, groups)
    out[...] = expand(full, lax.rem(i, per) * (lanes // span), lanes, span).reshape(3, 8, lanes)


def open_taps(fm, seg_col, lo, n):
    for j in range(1, SHORT):
        same = seg_col[pl.ds(lo, n), :] == seg_col[pl.ds(lo - j, n), :]
        fm[j - 1, pl.ds(0, n), :] = jnp.where(same, 1.0, 0.0)


def last_kernel(span, g, kv, ctaps, seg_col, out, fm, gs, taps):
    spread(ctaps, taps, span)
    rows = out.shape[1]
    more = rows + EDGE

    @pl.when(pl.program_id(0) == 0)
    def _():
        open_taps(fm, seg_col, EDGE, more)

    f32 = jnp.float32
    gs[0] = g[0].astype(f32)
    back = g[1].astype(f32)
    gs[1] = back * kv[1]
    gs[2] = back * kv[0]
    for t in range(out.shape[2] // LANES):
        at = pl.ds(t * LANES, LANES)
        for m in range(3):
            total = taps[m, 0:1, at] * gs[m, pl.ds(0, rows), at]
            for j in range(1, SHORT):
                total = total + taps[m, j : j + 1, at] * (
                    fm[j - 1, pl.ds(j, rows), :] * gs[m, pl.ds(j, rows), at])
            out[m, :, at] = total.astype(jnp.bfloat16)


def mix_kernel(chans, own, span, q, qprev, qnext, gown, gprev, gnext, cot, cnext, ctaps, filt, filt_rev, seg_col,
               seg_row, hy, out, xs, fm, mf, mb, lf, lt, gat, gl, sh, cs, sent, ssem, rsem, lsem):
    tile = pl.program_id(0)
    c, _ = spot()
    more = out.shape[1]
    rows_dev = more - EDGE
    width = out.shape[2] // chans
    grads = sent.at[tile]
    blocks = own // MEDIUM
    sizes = [MEDIUM] * blocks + [TAIL]
    grow = own + GROW
    f32 = jnp.float32

    def sends(t):
        place = out.at[:, :, pl.ds(pl.multiple_of(c * width + t * LANES, LANES), LANES)]
        part = lambda d: sent.at[t, :, pl.ds(pl.multiple_of(d * rows_dev, 8), more), :]
        made = []
        for k in range(1, chans):
            d = lax.rem(c + k, chans)
            made.append(remote(part(d), place, ssem.at[t, k], rsem.at[t, k], {"chan": d}))
        made.append(pltpu.make_async_copy(part(c), place, lsem.at[t]))
        return made

    @pl.when(tile == 0)
    def _():
        greet(chans, 0, False, False)
        open_taps(fm, seg_col, TAIL, grow)
        for b, rows in enumerate(sizes):
            r = lax.broadcasted_iota(jnp.int32, (rows, 2 * MEDIUM), 0)
            k = lax.broadcasted_iota(jnp.int32, (rows, 2 * MEDIUM), 1)
            here = jnp.tile(seg_col[pl.ds(TAIL + MEDIUM * b, rows), :], (1, 2))
            past = jnp.broadcast_to(seg_row[0:1, pl.ds(MEDIUM * b, 2 * MEDIUM)], (rows, 2 * MEDIUM))
            lag = r + MEDIUM - k
            ok = (lag >= 0) & (lag < MEDIUM) & (here == past)
            mf[b, pl.ds(0, rows), :] = jnp.where(ok, 1.0, 0.0).astype(jnp.bfloat16)
            ahead = jnp.broadcast_to(seg_row[0:1, pl.ds(MEDIUM * (b + 1), 2 * MEDIUM)], (rows, 2 * MEDIUM))
            lag = k - r
            ok = (lag >= 0) & (lag < MEDIUM) & (here == ahead)
            mb[b, pl.ds(0, rows), :] = jnp.where(ok, 1.0, 0.0).astype(jnp.bfloat16)
        gat[...] = jnp.zeros_like(gat)
        gl[...] = jnp.zeros_like(gl)

    xs[pl.ds(0, TAIL), :] = qprev[...].astype(f32)
    xs[pl.ds(TAIL, own), :] = q[...].astype(f32)
    xs[pl.ds(TAIL + own, GROW), :] = qnext[...].astype(f32)
    cs[pl.ds(0, own), :] = cot[...].astype(f32)
    cs[pl.ds(own, GROW), :] = cnext[...].astype(f32)
    gat[pl.ds(0, MEDIUM), :] = gprev[...]
    gat[pl.ds(MEDIUM, own), :] = gown[...]
    gat[pl.ds(MEDIUM + own, TAIL), :] = gnext[...]
    taps = expand(ctaps[0], tile * (LANES // span), LANES, span)
    coef = [taps[j : j + 1, :] for j in range(SHORT)]
    step = 80
    for at in range(0, grow, step):
        total = coef[0] * xs[pl.ds(TAIL + at, step), :]
        for j in range(1, SHORT):
            total = total + coef[j] * (fm[j - 1, pl.ds(at, step), :] * xs[pl.ds(TAIL + at - j, step), :])
        if at < own:
            n = min(step, own - at)
            sh[pl.ds(at, n), :] = total[:n]
        gl[pl.ds(at, step), :] = (cs[pl.ds(at, step), :] * total).astype(jnp.bfloat16)

    lane_group = lax.broadcasted_iota(jnp.int32, (MEDIUM, LANES), 1) // (LANES // 8)

    def band(filters, masks):
        for g in range(8):
            row = jnp.broadcast_to(filters[g : g + 1, :], (MEDIUM, MEDIUM))
            circ = pltpu.roll(row, 0, 1, stride=1, stride_axis=0).astype(jnp.bfloat16)
            two = jnp.concatenate([circ, circ], axis=1)
            for b in range(blocks):
                lf[b, pl.ds(g * MEDIUM, MEDIUM), :] = two * masks[b]
            lt[pl.ds(g * TAIL, TAIL), :] = two[:TAIL] * masks[blocks, pl.ds(0, TAIL), :]

    def product(b, source):
        rhs = source[pl.ds(MEDIUM * b, 2 * MEDIUM), :]
        rows = sizes[b]
        lhs = lf[b] if b < blocks else lt[...]
        res = jnp.dot(lhs, rhs, preferred_element_type=f32)
        total = res[:rows]
        for g in range(1, 8):
            total = jnp.where(lane_group[:rows] == g, res[g * rows : (g + 1) * rows], total)
        return total

    band(filt_rev, mf)
    for b, rows in enumerate(sizes):
        long = product(b, gat)
        at = pl.ds(MEDIUM * b, rows)
        if b < blocks:
            hy[at, :] = (sh[at, :] * long).astype(jnp.bfloat16)
        grads[0, at, :] = (cs[at, :] * long).astype(jnp.bfloat16)
    band(filt, mb)
    for b, rows in enumerate(sizes):
        grads[1, pl.ds(MEDIUM * b, rows), :] = product(b, gl).astype(jnp.bfloat16)

    for cp in sends(tile):
        cp.start()

    @pl.when(tile == pl.num_programs(0) - 1)
    def _():
        def finish(t, carry):
            for cp in sends(t):
                cp.wait()
            return carry

        lax.fori_loop(0, pl.num_programs(0), finish, 0)


def solution(mesh):
    chans, seqs = mesh.shape["chan"], mesh.shape["seq"]

    def body(features, cotangent, short_filter, medium_filter, doc_start):
        own, width = cotangent.shape
        rows, _, full = features.shape
        groups = medium_filter.shape[0]
        span = full // (groups * chans)
        grow = own + GROW
        more = rows + EDGE
        bf, f32 = jnp.bfloat16, jnp.float32
        shape = jax.ShapeDtypeStruct
        dma = pltpu.SemaphoreType.DMA
        x = jnp.transpose(features, (1, 0, 2))
        ctaps = jnp.pad(jnp.transpose(short_filter, (0, 2, 1)), ((0, 0), (0, 1), (0, 0)))
        wide = min(WIDE, width)
        limit = 60 << 20

        tokens = own * seqs
        bounds = jnp.arange(doc_start.shape[0], dtype=jnp.int32) * own + doc_start

        def ids(base, n):
            pos = base + jnp.arange(n, dtype=jnp.int32)
            seg = jnp.sum((bounds[None, :] <= pos[:, None]).astype(jnp.int32), axis=1)
            return jnp.where(pos < 0, -1, jnp.where(pos >= tokens, FAR, seg))

        start = lax.axis_index("seq") * own
        seg = ids(start - MEDIUM, own + 3 * MEDIUM)
        cols = TAIL + grow
        seg_col = jnp.broadcast_to(seg[MEDIUM - TAIL : MEDIUM - TAIL + cols, None], (cols, LANES))
        seg_row = jnp.broadcast_to(seg[None], (8, seg.shape[0]))
        rseg = ids(start + lax.axis_index("chan") * rows - EDGE, rows + 2 * EDGE)
        rseg_col = jnp.broadcast_to(rseg[:, None], (rseg.shape[0], LANES))
        filt = medium_filter.astype(bf).astype(f32)
        filt_rev = jnp.roll(filt[:, ::-1], 1, axis=1)

        whole = lambda dims: pl.BlockSpec(dims, lambda i: (0,) * len(dims))
        flat = lambda n, w: pl.BlockSpec((n, w), lambda i: (0, i))
        cube = lambda m, n, w: pl.BlockSpec((m, n, w), lambda i: (0, 0, i))
        pieces = chans * (width // wide)
        vmem = pl.BlockSpec(memory_space=pltpu.VMEM)
        parts = lambda n: shape((n, width), bf)
        q, taps, cnext, gown, gprev, gnext, qprev, qnext, kv = pl.pallas_call(
            functools.partial(front_kernel, chans, seqs, span, wide),
            out_shape=(
                parts(own), shape((chans, 3, 8, groups), f32), parts(GROW), parts(own), parts(MEDIUM), parts(TAIL),
                parts(TAIL), parts(GROW), shape((2, more, full), f32)),
            in_specs=[ANY, ANY, ANY, vmem],
            out_specs=(ANY, vmem) + (ANY,) * 7,
            scratch_shapes=[
                pltpu.VMEM((2, rows, full), bf), pltpu.VMEM((2, EDGE, full), bf), pltpu.VMEM((2, EDGE, full), bf),
                pltpu.VMEM((rows, full), bf), pltpu.VMEM((2, more, full), f32),
                pltpu.VMEM((SHORT - 1, more, LANES), f32), pltpu.VMEM((2, rows + 2 * EDGE, wide), f32),
                pltpu.VMEM((3, 8, wide), f32),
                dma((chans,)), dma((chans,)), dma((chans,)), dma((chans,)),
                dma((pieces,)), dma((pieces,)), dma((width // wide,)),
                dma((5 + 2 * (width // wide),)), dma((5 + 2 * (width // wide),)), dma((pieces,)), dma((3,)),
            ],
            compiler_params=pltpu.CompilerParams(
                collective_id=0, has_side_effects=True, vmem_limit_bytes=limit),
            name="front",
        )(x, cotangent, ctaps, rseg_col)

        blocks = own // MEDIUM
        tiles = width // LANES
        hy, back = pl.pallas_call(
            functools.partial(mix_kernel, chans, own, span),
            grid=(width // LANES,),
            out_shape=(shape((own, width), bf), shape((2, more, full), bf)),
            in_specs=[
                flat(own, LANES), flat(TAIL, LANES), flat(GROW, LANES),
                flat(own, LANES), flat(MEDIUM, LANES), flat(TAIL, LANES),
                flat(own, LANES), flat(GROW, LANES),
                whole((1, 8, groups)),
                pl.BlockSpec((8, MEDIUM), lambda i: (i, 0)),
                pl.BlockSpec((8, MEDIUM), lambda i: (i, 0)),
                whole(seg_col.shape), whole(seg_row.shape),
            ],
            out_specs=(flat(own, LANES), ANY),
            scratch_shapes=[
                pltpu.VMEM((cols, LANES), f32),
                pltpu.VMEM((SHORT - 1, grow, LANES), f32),
                pltpu.VMEM((blocks + 1, MEDIUM, 2 * MEDIUM), bf),
                pltpu.VMEM((blocks + 1, MEDIUM, 2 * MEDIUM), bf),
                pltpu.VMEM((blocks, 8 * MEDIUM, 2 * MEDIUM), bf),
                pltpu.VMEM((8 * TAIL, 2 * MEDIUM), bf),
                pltpu.VMEM((own + 2 * MEDIUM, LANES), bf),
                pltpu.VMEM((own + 2 * MEDIUM, LANES), bf),
                pltpu.VMEM((own, LANES), f32),
                pltpu.VMEM((grow, LANES), f32),
                pltpu.VMEM((tiles, 2, own + TAIL, LANES), bf),
                dma((tiles, chans)), dma((tiles, chans)), dma((tiles,)),
            ],
            compiler_params=pltpu.CompilerParams(
                collective_id=2, has_side_effects=True, vmem_limit_bytes=limit),
            name="mix_tile",
        )(q, qprev, qnext, gown, gprev, gnext, cotangent, cnext, ctaps[:1], filt, filt_rev, seg_col, seg_row)

        grad = pl.pallas_call(
            functools.partial(last_kernel, span),
            grid=(full // wide,),
            out_shape=shape((3, rows, full), bf),
            in_specs=[cube(2, more, wide), cube(2, more, wide), whole(taps.shape), whole(rseg_col.shape)],
            out_specs=cube(3, rows, wide),
            scratch_shapes=[pltpu.VMEM((SHORT - 1, more, LANES), f32), pltpu.VMEM((3, more, wide), f32),
                            pltpu.VMEM((3, 8, wide), f32)],
            compiler_params=pltpu.CompilerParams(vmem_limit_bytes=limit),
            name="last_rows",
        )(back, kv, taps, rseg_col)
        return hy, jnp.transpose(grad, (1, 0, 2))

    in_specs = (
        P(("seq", "chan"), None, None),
        P("seq", "chan"),
        P(None, "chan", None),
        P("chan", None),
        P(),
    )
    out_specs = (P("seq", "chan"), P(("seq", "chan"), None, None))
    return jax.shard_map(body, mesh=mesh, in_specs=in_specs, out_specs=out_specs, check_vma=False)
```
